32 devices in a mesh: ctx: 8 (over z, x), tp: 4 (over y, core).
Axes of the slice: x: 2, y: 2, z: 4, core: 2. Of those that a mesh axis runs over, the one named last changes fastest.
Arguments:
- features: bfloat16 [2048, 3, 4096], P('ctx', None, 'tp'), may hold values from -6 to 6
- short_filter: float32 [3, 3, 4096], P(None, None, 'tp'), may hold values from -3 to 3
- log_decay: float32 [16, 4096], P(None, 'tp'), may hold values from 0.00012207031 to 0.0333333333
- residue: float32 [16, 4096], P(None, 'tp'), may hold values from -0.52 to 0.52
- residual: bfloat16 [2048, 4096], P('ctx', 'tp'), may hold values from -6 to 6
- out_weight: bfloat16 [4096, 4096], P(('ctx', 'tp')), may hold values from -0.09375 to 0.09375
Outputs:
- mixed: bfloat16 [2048, 4096], P('ctx', 'tp')
The draws below stay inside these ranges and needn't reach their ends.
All inputs are finite; a program needn't handle non-finite values.
Results may differ from the reference program's by a relative error of at most 0.0048.
Values may be sent and summed in bfloat16 or wider, within the bound.
No kernel may reach another device: no remote copies, remote signals or barrier semaphores. Data moves between devices by JAX's collectives and lax.ppermute only.
A program may use at most 128 MiB of HBM per device.

```python
import jax
import jax.numpy as jnp
from jax import lax

D = 4096
M = 16
KS = 3
TOKENS = 2048


def modal_tables(key):
    base = jax.random.fold_in(key, 11)
    category = jax.random.uniform(jax.random.fold_in(base, 1), (M, D))
    uniform_pos = jax.random.uniform(jax.random.fold_in(base, 2), (M, D))

    def log_between(low_end, high_end):
        return jnp.exp(jnp.log(low_end) + uniform_pos * (jnp.log(high_end) - jnp.log(low_end)))
    slow_rates = log_between(0.25 / TOKENS, 2.0 / TOKENS)
    middle_rates = log_between(2.0 / TOKENS, 0.02)
    fast_rates = log_between(0.02, 1.0 / 30.0)
    slow_share = 0.5
    middle_share = 0.75
    rates_out = jnp.where(category < slow_share, slow_rates, jnp.where(category < middle_share, middle_rates, fast_rates))
    normal_part = jnp.clip(jax.random.normal(jax.random.fold_in(base, 3), (M, D)), -4.0, 4.0)
    residues = normal_part * jnp.sqrt(2.0 * rates_out) * 0.5
    return (rates_out.astype(jnp.float32), residues.astype(jnp.float32))


def draw_log_decay(key, part):
    return modal_tables(key)[0]


def draw_residue(key, part):
    return modal_tables(key)[1]


def block_scale(stream_key, extent, split, low, largest):
    def one(position, blocks):
        draws = jax.random.uniform(jax.random.fold_in(jax.random.fold_in(stream_key, 6), position), (blocks,), jnp.float32, low / len(split), largest / len(split))
        return jnp.repeat(jnp.exp(draws), extent[position] // blocks).reshape((-1,) + (1,) * (len(extent) - position - 1))

    level = one(*split[0])
    for cut in split[1:]:
        level = level * one(*cut)
    return level


def centred(rng, shape, width, bound, split=(), dtype=jnp.bfloat16):
    level = block_scale(rng, shape, split, -0.22, 0.18) if split else 1.0
    array = jax.random.normal(rng, shape, jnp.float32) * width * level
    return jnp.minimum(jnp.maximum(array, -bound), bound).astype(dtype)


def setup_inputs(seed: int = 0) -> dict:
    streams_of = jax.random.split(jax.random.key(seed), 7)
    features = centred(streams_of[0], (TOKENS, 3, D), 1.0, 6.0, ((0, 8), (2, 4)))
    short_filter = centred(streams_of[1], (3, KS, D), 0.6, 3.0, ((2, 4),), jnp.float32)
    log_decay = draw_log_decay(jax.random.fold_in(streams_of[6], 71), 0)
    residue = draw_residue(jax.random.fold_in(streams_of[6], 71), 0)
    residual = centred(streams_of[4], (TOKENS, D), 1.0, 6.0, ((0, 8), (1, 4)))
    out_weight = centred(streams_of[5], (D, D), D ** -0.5, 0.09375, ((0, 32),))
    return {"features": features, "short_filter": short_filter, "log_decay": log_decay, "residue": residue, "residual": residual, "out_weight": out_weight}


def reference(features, short_filter, log_decay, residue, residual, out_weight):
    streams = features.astype(jnp.float32)
    padded_in = jnp.pad(streams, ((KS - 1, 0), (0, 0), (0, 0)))
    filtered = jnp.zeros(streams.shape, jnp.float32)
    for tap_idx in range(KS):
        filtered = filtered + short_filter[:, tap_idx, :][None] * padded_in[KS - 1 - tap_idx: KS - 1 - tap_idx + TOKENS]
    gate_q = filtered[:, 0, :]
    driven = filtered[:, 1, :] * filtered[:, 2, :]
    decay_per = jnp.exp(-log_decay)

    def advance(modal_state, driven_row):
        modal_state = decay_per * modal_state + driven_row[None, :]
        return modal_state, jnp.sum(residue * modal_state, axis=0)

    _, long_out = lax.scan(advance, jnp.zeros((M, D), jnp.float32), driven)
    gated = (gate_q * long_out).astype(jnp.bfloat16)
    projected = jnp.dot(gated, out_weight, preferred_element_type=jnp.float32)
    return (residual.astype(jnp.float32) + projected).astype(jnp.bfloat16)
```

```python
import functools

import jax
import jax.numpy as jnp
from jax import lax
from jax.experimental import pallas as pl
from jax.experimental.pallas import tpu as pltpu
from jax.sharding import PartitionSpec as P

LANES = 128
SEGS = 8


def row(ref_value, n):
    return jnp.broadcast_to(ref_value[n : n + 1, :], (SEGS, ref_value.shape[1]))


def shifted(value, halo_row):
    lane_row = lax.broadcasted_iota(jnp.int32, value.shape, 0)
    return jnp.where(lane_row == 0, halo_row, pltpu.roll(value, 1, 0))


def history(tokens, halo, stream, lanes, seg_len, filter_len):
    rim = halo[stream, :, lanes].astype(jnp.float32)
    past = []
    for back in range(1, filter_len):
        last = tokens[pl.ds(seg_len - back, SEGS, stride=seg_len), :]
        past.append(shifted(last, rim[filter_len - 1 - back : filter_len - back, :]))
    return past


def taps_of(taps, stream, lanes, filter_len):
    values = taps[stream, :, lanes]
    return [row(values, j) for j in range(filter_len)]


def filter_step(now, past, taps):
    total = taps[0] * now
    for tap, old in zip(taps[1:], past):
        total = total + tap * old
    return total, [now] + past[:-1]


def scan_kernel(
    seg_len, feats, halo, taps, decay, driven, end, before, k_rows, v_rows
):
    modes, channels = decay.shape
    filter_len = taps.shape[1]
    seg = lax.broadcasted_iota(jnp.int32, (SEGS, LANES), 0)

    def one_group(group, _):
        lanes = pl.ds(pl.multiple_of(group * LANES, LANES), LANES)
        rate = decay[:, lanes]
        per_token = jnp.exp(-rate)
        step = [row(per_token, n) for n in range(modes)]
        k_rows[...] = feats[1, :, lanes].astype(jnp.float32)
        v_rows[...] = feats[2, :, lanes].astype(jnp.float32)
        k_taps = taps_of(taps, 1, lanes, filter_len)
        v_taps = taps_of(taps, 2, lanes, filter_len)

        def one_token(i, carry):
            states, k_past, v_past = carry
            at = pl.ds(i, SEGS, stride=seg_len)
            k, k_past = filter_step(k_rows[at, :], k_past, k_taps)
            v, v_past = filter_step(v_rows[at, :], v_past, v_taps)
            drive = k * v
            driven[i, :, lanes] = drive
            states = [a * s + drive for a, s in zip(step, states)]
            return states, k_past, v_past

        zero = jnp.zeros((SEGS, LANES), jnp.float32)
        states, _, _ = lax.fori_loop(
            0,
            seg_len,
            one_token,
            (
                [zero] * modes,
                history(k_rows, halo, 1, lanes, seg_len, filter_len),
                history(v_rows, halo, 2, lanes, seg_len, filter_len),
            ),
            unroll=4,
        )
        hop = 1
        while hop < SEGS:
            weight = jnp.exp(-rate * float(seg_len * hop))
            states = [
                s + row(weight, n) * jnp.where(seg >= hop, pltpu.roll(s, hop, 0), 0.0)
                for n, s in enumerate(states)
            ]
            hop *= 2
        for n, s in enumerate(states):
            end[n : n + 1, lanes] = s[SEGS - 1 :, :]
            before[n, :, lanes] = jnp.where(seg >= 1, pltpu.roll(s, 1, 0), 0.0)
        return 0

    lax.fori_loop(0, channels // LANES, one_group, 0)


def output_kernel(
    seg_len, parts, feats, halo, taps, decay, residue, driven, before, incoming, out, rows, q_rows
):
    modes, channels = decay.shape
    filter_len = taps.shape[1]
    seg = lax.broadcasted_iota(jnp.int32, (SEGS, LANES), 0).astype(jnp.float32)

    def one_group(group, _):
        lanes = pl.ds(pl.multiple_of(group * LANES, LANES), LANES)
        rate = decay[:, lanes]
        per_token = jnp.exp(-rate)
        weights = residue[:, lanes]
        entering = incoming[:, lanes]
        step = [row(per_token, n) for n in range(modes)]
        gain = [row(weights, n) for n in range(modes)]
        q_rows[...] = feats[0, :, lanes].astype(jnp.float32)
        q_taps = taps_of(taps, 0, lanes, filter_len)
        states = [
            before[n, :, lanes]
            + jnp.exp(-row(rate, n) * (seg * float(seg_len))) * row(entering, n)
            for n in range(modes)
        ]

        def one_token(i, carry):
            states, q_past = carry
            at = pl.ds(i, SEGS, stride=seg_len)
            gate, q_past = filter_step(q_rows[at, :], q_past, q_taps)
            drive = driven[i, :, lanes]
            states = [a * s + drive for a, s in zip(step, states)]
            terms = [r * s for r, s in zip(gain, states)]
            while len(terms) > 1:
                terms = [a + b for a, b in zip(terms[::2], terms[1::2])]
            rows[at, :] = gate * terms[0]
            return states, q_past

        lax.fori_loop(
            0,
            seg_len,
            one_token,
            (states, history(q_rows, halo, 0, lanes, seg_len, filter_len)),
            unroll=4,
        )
        place = pl.ds(pl.multiple_of((group // parts) * LANES, LANES), LANES)
        out[group % parts, :, place] = rows[...].astype(jnp.bfloat16)
        return 0

    lax.fori_loop(0, channels // LANES, one_group, 0)


def vmem(count):
    return [pl.BlockSpec(memory_space=pltpu.VMEM)] * count


def flip(value, axis, bit):
    count = lax.axis_size(axis)
    return lax.ppermute(value, axis, [(i, i ^ bit) for i in range(count)])


def entering_state(end, log_decay, tok_rows):
    place = lax.axis_index("ctx")
    count = lax.axis_size("ctx")
    prefix = jnp.zeros_like(end)
    total = end
    bit = 1
    while bit < count:
        other = flip(total, "ctx", bit)
        upper = (place & bit) != 0
        covered = (place & (bit - 1)).astype(jnp.float32) * float(tok_rows)
        prefix = prefix + jnp.where(upper, jnp.exp(-log_decay * covered) * other, 0.0)
        first = jnp.where(upper, other, total)
        second = jnp.where(upper, total, other)
        total = jnp.exp(-log_decay * float(tok_rows * bit)) * first + second
        bit *= 2
    return prefix


def gated_blocks(features, short_filter, log_decay, residue, parts):
    tok_rows, streams, channels = features.shape
    filter_len = short_filter.shape[1]
    modes = log_decay.shape[0]
    seg_len = tok_rows // SEGS
    count = lax.axis_size("ctx")
    rim = lax.ppermute(
        features[tok_rows - (filter_len - 1) :],
        "ctx",
        [(i, i + 1) for i in range(count - 1)],
    )
    feats = jnp.transpose(features, (1, 0, 2))
    halo = jnp.transpose(rim, (1, 0, 2))
    driven, end, before = pl.pallas_call(
        functools.partial(scan_kernel, seg_len),
        out_shape=(
            jax.ShapeDtypeStruct((seg_len, SEGS, channels), jnp.float32),
            jax.ShapeDtypeStruct((modes, channels), jnp.float32),
            jax.ShapeDtypeStruct((modes, SEGS, channels), jnp.float32),
        ),
        in_specs=vmem(4),
        out_specs=tuple(vmem(3)),
        scratch_shapes=[pltpu.VMEM((tok_rows, LANES), jnp.float32)] * 2,
        name="scan_ends",
    )(feats, halo, short_filter, log_decay)
    incoming = entering_state(end, log_decay, tok_rows)
    return pl.pallas_call(
        functools.partial(output_kernel, seg_len, parts),
        out_shape=jax.ShapeDtypeStruct((parts, tok_rows, channels // parts), jnp.bfloat16),
        in_specs=vmem(8),
        out_specs=vmem(1)[0],
        scratch_shapes=[pltpu.VMEM((tok_rows, LANES), jnp.float32)] * 2,
        name="gated_rows",
    )(feats, halo, short_filter, log_decay, residue, driven, before, incoming)


def project_gathered(gated, residual, out_weight):
    columns = lax.all_to_all(out_weight, "tp", split_axis=1, concat_axis=0, tiled=True)
    weight = lax.all_gather(columns, "ctx", axis=0, tiled=True)
    rows = lax.all_gather(gated, "tp", axis=1, tiled=True)
    projected = jnp.dot(rows, weight, preferred_element_type=jnp.float32)
    return (residual.astype(jnp.float32) + projected).astype(jnp.bfloat16)


def on_device(features, short_filter, log_decay, residue, residual, out_weight):
    gated = gated_blocks(features, short_filter, log_decay, residue, 1)[0]
    return project_gathered(gated, residual, out_weight)


def solution(mesh):
    return jax.shard_map(
        on_device,
        mesh=mesh,
        in_specs=(
            P("ctx", None, "tp"),
            P(None, None, "tp"),
            P(None, "tp"),
            P(None, "tp"),
            P("ctx", "tp"),
            P(("ctx", "tp"), None),
        ),
        out_specs=P("ctx", "tp"),
        check_vma=False,
    )
```

```python
import functools

import jax
import jax.numpy as jnp
from jax import lax
from jax.experimental import pallas as pl
from jax.experimental.pallas import tpu as pltpu
from jax.sharding import PartitionSpec as P

LANES = 128
CHUNKS = 2
SEGS = 8


def row(ref_value, n):
    return jnp.broadcast_to(ref_value[n : n + 1, :], (SEGS, ref_value.shape[1]))


def shifted(value, halo_row):
    lane_row = lax.broadcasted_iota(jnp.int32, value.shape, 0)
    return jnp.where(lane_row == 0, halo_row, pltpu.roll(value, 1, 0))


def history(tokens, halo, stream, lanes, seg_len, filter_len):
    rim = halo[stream, :, lanes].astype(jnp.float32)
    past = []
    for back in range(1, filter_len):
        last = tokens[pl.ds(seg_len - back, SEGS, stride=seg_len), :]
        past.append(shifted(last, rim[filter_len - 1 - back : filter_len - back, :]))
    return past


def taps_of(taps, stream, lanes, filter_len):
    values = taps[stream, :, lanes]
    return [row(values, j) for j in range(filter_len)]


def filter_step(now, past, taps):
    total = taps[0] * now
    for tap, old in zip(taps[1:], past):
        total = total + tap * old
    return total, [now] + past[:-1]


def scan_kernel(
    seg_len, feats, halo, taps, decay, driven, end, before, k_rows, v_rows
):
    modes, channels = decay.shape
    filter_len = taps.shape[1]
    seg = lax.broadcasted_iota(jnp.int32, (SEGS, LANES), 0)

    def one_group(group, _):
        lanes = pl.ds(pl.multiple_of(group * LANES, LANES), LANES)
        rate = decay[:, lanes]
        per_token = jnp.exp(-rate)
        step = [row(per_token, n) for n in range(modes)]
        k_rows[...] = feats[1, :, lanes].astype(jnp.float32)
        v_rows[...] = feats[2, :, lanes].astype(jnp.float32)
        k_taps = taps_of(taps, 1, lanes, filter_len)
        v_taps = taps_of(taps, 2, lanes, filter_len)

        def one_token(i, carry):
            states, k_past, v_past = carry
            at = pl.ds(i, SEGS, stride=seg_len)
            k, k_past = filter_step(k_rows[at, :], k_past, k_taps)
            v, v_past = filter_step(v_rows[at, :], v_past, v_taps)
            drive = k * v
            driven[i, :, lanes] = drive
            states = [a * s + drive for a, s in zip(step, states)]
            return states, k_past, v_past

        zero = jnp.zeros((SEGS, LANES), jnp.float32)
        states, _, _ = lax.fori_loop(
            0,
            seg_len,
            one_token,
            (
                [zero] * modes,
                history(k_rows, halo, 1, lanes, seg_len, filter_len),
                history(v_rows, halo, 2, lanes, seg_len, filter_len),
            ),
            unroll=4,
        )
        hop = 1
        while hop < SEGS:
            weight = jnp.exp(-rate * float(seg_len * hop))
            states = [
                s + row(weight, n) * jnp.where(seg >= hop, pltpu.roll(s, hop, 0), 0.0)
                for n, s in enumerate(states)
            ]
            hop *= 2
        for n, s in enumerate(states):
            end[n : n + 1, lanes] = s[SEGS - 1 :, :]
            before[n, :, lanes] = jnp.where(seg >= 1, pltpu.roll(s, 1, 0), 0.0)
        return 0

    lax.fori_loop(0, channels // LANES, one_group, 0)


def output_kernel(
    seg_len, parts, feats, halo, taps, decay, residue, driven, before, incoming, out, rows, q_rows
):
    modes, channels = decay.shape
    filter_len = taps.shape[1]
    seg = lax.broadcasted_iota(jnp.int32, (SEGS, LANES), 0).astype(jnp.float32)

    def one_group(group, _):
        lanes = pl.ds(pl.multiple_of(group * LANES, LANES), LANES)
        rate = decay[:, lanes]
        per_token = jnp.exp(-rate)
        weights = residue[:, lanes]
        entering = incoming[:, lanes]
        step = [row(per_token, n) for n in range(modes)]
        gain = [row(weights, n) for n in range(modes)]
        q_rows[...] = feats[0, :, lanes].astype(jnp.float32)
        q_taps = taps_of(taps, 0, lanes, filter_len)
        states = [
            before[n, :, lanes]
            + jnp.exp(-row(rate, n) * (seg * float(seg_len))) * row(entering, n)
            for n in range(modes)
        ]

        def one_token(i, carry):
            states, q_past = carry
            at = pl.ds(i, SEGS, stride=seg_len)
            gate, q_past = filter_step(q_rows[at, :], q_past, q_taps)
            drive = driven[i, :, lanes]
            states = [a * s + drive for a, s in zip(step, states)]
            terms = [r * s for r, s in zip(gain, states)]
            while len(terms) > 1:
                terms = [a + b for a, b in zip(terms[::2], terms[1::2])]
            rows[at, :] = gate * terms[0]
            return states, q_past

        lax.fori_loop(
            0,
            seg_len,
            one_token,
            (states, history(q_rows, halo, 0, lanes, seg_len, filter_len)),
            unroll=4,
        )
        place = pl.ds(pl.multiple_of((group // parts) * LANES, LANES), LANES)
        out[group % parts, :, place] = rows[...].astype(jnp.bfloat16)
        return 0

    lax.fori_loop(0, channels // LANES, one_group, 0)


def vmem(count):
    return [pl.BlockSpec(memory_space=pltpu.VMEM)] * count


def flip(value, axis, bit):
    count = lax.axis_size(axis)
    return lax.ppermute(value, axis, [(i, i ^ bit) for i in range(count)])


def entering_state(end, log_decay, tok_rows):
    place = lax.axis_index("ctx")
    count = lax.axis_size("ctx")
    prefix = jnp.zeros_like(end)
    total = end
    bit = 1
    while bit < count:
        other = flip(total, "ctx", bit)
        upper = (place & bit) != 0
        covered = (place & (bit - 1)).astype(jnp.float32) * float(tok_rows)
        prefix = prefix + jnp.where(upper, jnp.exp(-log_decay * covered) * other, 0.0)
        first = jnp.where(upper, other, total)
        second = jnp.where(upper, total, other)
        total = jnp.exp(-log_decay * float(tok_rows * bit)) * first + second
        bit *= 2
    return prefix


def gated_blocks(features, short_filter, log_decay, residue, parts):
    tok_rows, streams, channels = features.shape
    filter_len = short_filter.shape[1]
    modes = log_decay.shape[0]
    seg_len = tok_rows // SEGS
    count = lax.axis_size("ctx")
    rim = lax.ppermute(
        features[tok_rows - (filter_len - 1) :],
        "ctx",
        [(i, i + 1) for i in range(count - 1)],
    )
    feats = jnp.transpose(features, (1, 0, 2))
    halo = jnp.transpose(rim, (1, 0, 2))
    driven, end, before = pl.pallas_call(
        functools.partial(scan_kernel, seg_len),
        out_shape=(
            jax.ShapeDtypeStruct((seg_len, SEGS, channels), jnp.float32),
            jax.ShapeDtypeStruct((modes, channels), jnp.float32),
            jax.ShapeDtypeStruct((modes, SEGS, channels), jnp.float32),
        ),
        in_specs=vmem(4),
        out_specs=tuple(vmem(3)),
        scratch_shapes=[pltpu.VMEM((tok_rows, LANES), jnp.float32)] * 2,
        name="scan_ends",
    )(feats, halo, short_filter, log_decay)
    incoming = entering_state(end, log_decay, tok_rows)
    return pl.pallas_call(
        functools.partial(output_kernel, seg_len, parts),
        out_shape=jax.ShapeDtypeStruct((parts, tok_rows, channels // parts), jnp.bfloat16),
        in_specs=vmem(8),
        out_specs=vmem(1)[0],
        scratch_shapes=[pltpu.VMEM((tok_rows, LANES), jnp.float32)] * 2,
        name="gated_rows",
    )(feats, halo, short_filter, log_decay, residue, driven, before, incoming)


def project_gathered(gated, residual, out_weight):
    columns = lax.all_to_all(out_weight, "tp", split_axis=1, concat_axis=0, tiled=True)
    weight = lax.all_gather(columns, "ctx", axis=0, tiled=True)
    rows = lax.all_gather(gated, "tp", axis=1, tiled=True)
    projected = jnp.dot(rows, weight, preferred_element_type=jnp.float32)
    return (residual.astype(jnp.float32) + projected).astype(jnp.bfloat16)


def cube_kernel(
    piece, flags, own_c, own_o, other_c, other_o, *refs
):
    weights, (theirs, mine, left) = refs[:8], refs[8:]
    tile = pl.program_id(0)
    half = pl.num_programs(0) // 2
    x, y, same = flags[1], flags[2], flags[3]
    rows = own_c.shape[0]

    @pl.when(tile == 0)
    def _():
        def fill(plane, token, source):
            for xr in range(2):
                for yr in range(2):
                    at = jnp.bitwise_xor(x, xr) * 2 + jnp.bitwise_xor(y, yr)
                    place = ((plane * 2 + xr) * 2 + yr) * piece
                    left[pl.ds(token * rows, rows), pl.ds(place, piece)] = source[
                        :, pl.ds(pl.multiple_of(at * piece, piece), piece)
                    ]

        @pl.when(same == 1)
        def _():
            fill(0, 0, own_c)
            fill(0, 1, own_o)
            fill(1, 0, other_c)
            fill(1, 1, other_o)

        @pl.when(same == 0)
        def _():
            fill(0, 0, other_c)
            fill(0, 1, other_o)
            fill(1, 0, own_c)
            fill(1, 1, own_o)

    right = jnp.concatenate([w[...] for w in weights], axis=0)
    total = jnp.dot(left[...], right, preferred_element_type=jnp.float32)

    @pl.when(tile < half)
    def _():
        theirs[...] = total.astype(jnp.bfloat16)

    @pl.when(tile >= half)
    def _():
        mine[...] = total


def cube_product(flags, gated, weights, piece):
    rows = gated[0].shape[0]
    width = weights[0].shape[1] // 2
    tile = min(width, 256)
    half = width // tile

    def weight_at(i, flags):
        core = jnp.where(i < half, 1 - flags[0], flags[0])
        return (0, core * half + lax.rem(i, half))

    whole = pl.BlockSpec(gated[0].shape, lambda i, flags: (0, 0))
    return pl.pallas_call(
        functools.partial(cube_kernel, piece),
        out_shape=(
            jax.ShapeDtypeStruct((2 * rows, width), jnp.bfloat16),
            jax.ShapeDtypeStruct((2 * rows, width), jnp.float32),
        ),
        grid_spec=pltpu.PrefetchScalarGridSpec(
            num_scalar_prefetch=1,
            grid=(2 * half,),
            in_specs=[whole] * 4 + [pl.BlockSpec((piece, tile), weight_at)] * 8,
            out_specs=(
                pl.BlockSpec((2 * rows, tile), lambda i, flags: (0, jnp.minimum(i, half - 1))),
                pl.BlockSpec((2 * rows, tile), lambda i, flags: (0, jnp.maximum(i - half, 0))),
            ),
            scratch_shapes=[pltpu.VMEM((2 * rows, 8 * piece), jnp.bfloat16)],
        ),
        name="cube_product",
    )(flags, *gated, *weights)


def project_cube(gated, residual, out_weight, chunks):
    ctx, tp = lax.axis_size("ctx"), lax.axis_size("tp")
    c, t = lax.axis_index("ctx"), lax.axis_index("tp")
    core, y = t & 1, t >> 1
    x, zp, zh = c & 1, (c >> 1) & 1, c >> 2
    piece, columns = out_weight.shape
    channels = columns // tp
    width = channels // chunks

    def half(side, j):
        starts = [(2 * side + k) * channels + j * width for k in range(2)]
        return jnp.concatenate([out_weight[:, at : at + width] for at in starts], axis=1)

    keep = [jnp.where(y == 0, half(0, j), half(1, j)) for j in range(chunks)]
    give = [jnp.where(y == 0, half(1, j), half(0, j)) for j in range(chunks)]
    take = [flip(g, "tp", 2) for g in give]
    weights = []
    for j in range(chunks):
        near = [keep[j], take[j]]
        far = [flip(w, "ctx", 4) for w in near]
        weights.append(
            near + [flip(w, "ctx", 1) for w in near] + far + [flip(w, "ctx", 1) for w in far]
        )

    mine = jnp.where(core == 0, gated[0], gated[1])
    sib = jnp.where(core == 0, gated[1], gated[0])
    stays = core == zp
    pairs_q, pairs_r = [], []
    for ci in range(ctx):
        for ti in range(tp):
            if (ti & 1) == ((ci >> 1) & 1):
                pairs_q.append((ci * tp + ti, ci * tp + (ti ^ 1)))
            else:
                pairs_q.append((ci * tp + ti, (ci ^ 2) * tp + ti))
                pairs_r.append((ci * tp + ti, (ci ^ 2) * tp + (ti ^ 1)))
    q = lax.ppermute(jnp.where(stays, sib, mine), ("ctx", "tp"), pairs_q)
    r = lax.ppermute(sib, ("ctx", "tp"), pairs_r)
    own_c = jnp.where(stays, mine, q)
    own_o = jnp.where(stays, q, r)
    other_c = flip(own_c, "tp", 2)
    other_o = flip(own_o, "tp", 2)
    flags = jnp.stack([core, x, y, (y == zh).astype(jnp.int32)]).astype(jnp.int32)

    rows = residual.shape[0]
    outs = []
    for j in range(chunks):
        theirs, ours = cube_product(flags, (own_c, own_o, other_c, other_o), weights[j], piece)
        total = ours + flip(theirs, "tp", 1).astype(jnp.float32)
        pair = flip(total[rows:].astype(jnp.bfloat16), "ctx", 2)
        base = residual[:, j * width : (j + 1) * width].astype(jnp.float32)
        outs.append((base + (total[:rows] + pair.astype(jnp.float32))).astype(jnp.bfloat16))
    return jnp.concatenate(outs, axis=1)


def on_device(features, short_filter, log_decay, residue, residual, out_weight):
    ctx, tp = lax.axis_size("ctx"), lax.axis_size("tp")
    piece = out_weight.shape[0]
    if tp == 4 and ctx == 2 * tp and piece == LANES:
        gated = gated_blocks(features, short_filter, log_decay, residue, 2)
        return project_cube(gated, residual, out_weight, CHUNKS)
    gated = gated_blocks(features, short_filter, log_decay, residue, 1)[0]
    return project_gathered(gated, residual, out_weight)


def solution(mesh):
    return jax.shard_map(
        on_device,
        mesh=mesh,
        in_specs=(
            P("ctx", None, "tp"),
            P(None, None, "tp"),
            P(None, "tp"),
            P(None, "tp"),
            P("ctx", "tp"),
            P(("ctx", "tp"), None),
        ),
        out_specs=P("ctx", "tp"),
        check_vma=False,
    )
```

```python
import functools

import jax
import jax.numpy as jnp
from jax import lax
from jax.experimental import pallas as pl
from jax.experimental.pallas import tpu as pltpu
from jax.sharding import PartitionSpec as P


LANES = 128
CHUNKS = 2
SEGS = 8


def row(ref_value, n):
    return jnp.broadcast_to(ref_value[n : n + 1, :], (SEGS, ref_value.shape[1]))


def shifted(value, halo_row):
    lane_row = lax.broadcasted_iota(jnp.int32, value.shape, 0)
    return jnp.where(lane_row == 0, halo_row, pltpu.roll(value, 1, 0))


def history(tokens, halo, stream, lanes, seg_len, filter_len):
    rim = halo[stream, :, lanes].astype(jnp.float32)
    past = []
    for back in range(1, filter_len):
        last = tokens[pl.ds(seg_len - back, SEGS, stride=seg_len), :]
        past.append(shifted(last, rim[filter_len - 1 - back : filter_len - back, :]))
    return past


def taps_of(taps, stream, lanes, filter_len):
    values = taps[stream, :, lanes]
    return [row(values, j) for j in range(filter_len)]


def filter_step(now, past, taps):
    total = taps[0] * now
    for tap, old in zip(taps[1:], past):
        total = total + tap * old
    return total, [now] + past[:-1]


def scan_kernel(
    seg_len, feats, halo, taps, decay, driven, end, before, k_rows, v_rows
):
    modes, channels = decay.shape
    filter_len = taps.shape[1]
    seg = lax.broadcasted_iota(jnp.int32, (SEGS, LANES), 0)

    def one_group(group, _):
        lanes = pl.ds(pl.multiple_of(group * LANES, LANES), LANES)
        rate = decay[:, lanes]
        per_token = jnp.exp(-rate)
        step = [row(per_token, n) for n in range(modes)]
        k_rows[...] = feats[1, :, lanes].astype(jnp.float32)
        v_rows[...] = feats[2, :, lanes].astype(jnp.float32)
        k_taps = taps_of(taps, 1, lanes, filter_len)
        v_taps = taps_of(taps, 2, lanes, filter_len)

        def one_token(i, carry):
            states, k_past, v_past = carry
            at = pl.ds(i, SEGS, stride=seg_len)
            k, k_past = filter_step(k_rows[at, :], k_past, k_taps)
            v, v_past = filter_step(v_rows[at, :], v_past, v_taps)
            drive = k * v
            driven[i, :, lanes] = drive
            states = [a * s + drive for a, s in zip(step, states)]
            return states, k_past, v_past

        zero = jnp.zeros((SEGS, LANES), jnp.float32)
        states, _, _ = lax.fori_loop(
            0,
            seg_len,
            one_token,
            (
                [zero] * modes,
                history(k_rows, halo, 1, lanes, seg_len, filter_len),
                history(v_rows, halo, 2, lanes, seg_len, filter_len),
            ),
            unroll=4,
        )
        hop = 1
        while hop < SEGS:
            weight = jnp.exp(-rate * float(seg_len * hop))
            states = [
                s + row(weight, n) * jnp.where(seg >= hop, pltpu.roll(s, hop, 0), 0.0)
                for n, s in enumerate(states)
            ]
            hop *= 2
        for n, s in enumerate(states):
            end[n : n + 1, lanes] = s[SEGS - 1 :, :]
            before[n, :, lanes] = jnp.where(seg >= 1, pltpu.roll(s, 1, 0), 0.0)
        return 0

    lax.fori_loop(0, channels // LANES, one_group, 0)


def output_kernel(
    seg_len, parts, feats, halo, taps, decay, residue, driven, before, incoming, out, rows, q_rows
):
    modes, channels = decay.shape
    filter_len = taps.shape[1]
    seg = lax.broadcasted_iota(jnp.int32, (SEGS, LANES), 0).astype(jnp.float32)

    def one_group(group, _):
        lanes = pl.ds(pl.multiple_of(group * LANES, LANES), LANES)
        rate = decay[:, lanes]
        per_token = jnp.exp(-rate)
        weights = residue[:, lanes]
        entering = incoming[:, lanes]
        step = [row(per_token, n) for n in range(modes)]
        gain = [row(weights, n) for n in range(modes)]
        q_rows[...] = feats[0, :, lanes].astype(jnp.float32)
        q_taps = taps_of(taps, 0, lanes, filter_len)
        states = [
            before[n, :, lanes]
            + jnp.exp(-row(rate, n) * (seg * float(seg_len))) * row(entering, n)
            for n in range(modes)
        ]

        def one_token(i, carry):
            states, q_past = carry
            at = pl.ds(i, SEGS, stride=seg_len)
            gate, q_past = filter_step(q_rows[at, :], q_past, q_taps)
            drive = driven[i, :, lanes]
            states = [a * s + drive for a, s in zip(step, states)]
            terms = [r * s for r, s in zip(gain, states)]
            while len(terms) > 1:
                terms = [a + b for a, b in zip(terms[::2], terms[1::2])]
            rows[at, :] = gate * terms[0]
            return states, q_past

        lax.fori_loop(
            0,
            seg_len,
            one_token,
            (states, history(q_rows, halo, 0, lanes, seg_len, filter_len)),
            unroll=4,
        )
        place = pl.ds(pl.multiple_of((group // parts) * LANES, LANES), LANES)
        out[group % parts, :, place] = rows[...].astype(jnp.bfloat16)
        return 0

    lax.fori_loop(0, channels // LANES, one_group, 0)


def vmem(count):
    return [pl.BlockSpec(memory_space=pltpu.VMEM)] * count


def flip(value, axis, bit):
    count = lax.axis_size(axis)
    return lax.ppermute(value, axis, [(i, i ^ bit) for i in range(count)])


def entering_state(end, log_decay, tok_rows):
    place = lax.axis_index("ctx")
    count = lax.axis_size("ctx")
    prefix = jnp.zeros_like(end)
    total = end
    bit = 1
    while bit < count:
        other = flip(total, "ctx", bit)
        upper = (place & bit) != 0
        covered = (place & (bit - 1)).astype(jnp.float32) * float(tok_rows)
        prefix = prefix + jnp.where(upper, jnp.exp(-log_decay * covered) * other, 0.0)
        first = jnp.where(upper, other, total)
        second = jnp.where(upper, total, other)
        total = jnp.exp(-log_decay * float(tok_rows * bit)) * first + second
        bit *= 2
    return prefix


def gated_blocks(features, short_filter, log_decay, residue, parts):
    tok_rows, _, channels = features.shape
    filter_len = short_filter.shape[1]
    modes = log_decay.shape[0]
    seg_len = tok_rows // SEGS
    count = lax.axis_size("ctx")
    rim = lax.ppermute(
        features[tok_rows - (filter_len - 1) :],
        "ctx",
        [(i, i + 1) for i in range(count - 1)],
    )
    feats = jnp.transpose(features, (1, 0, 2))
    halo = jnp.transpose(rim, (1, 0, 2))
    driven, end, before = pl.pallas_call(
        functools.partial(scan_kernel, seg_len),
        out_shape=(
            jax.ShapeDtypeStruct((seg_len, SEGS, channels), jnp.float32),
            jax.ShapeDtypeStruct((modes, channels), jnp.float32),
            jax.ShapeDtypeStruct((modes, SEGS, channels), jnp.float32),
        ),
        in_specs=vmem(4),
        out_specs=tuple(vmem(3)),
        scratch_shapes=[pltpu.VMEM((tok_rows, LANES), jnp.float32)] * 2,
        name="scan_ends",
    )(feats, halo, short_filter, log_decay)
    incoming = entering_state(end, log_decay, tok_rows)
    return pl.pallas_call(
        functools.partial(output_kernel, seg_len, parts),
        out_shape=jax.ShapeDtypeStruct((parts, tok_rows, channels // parts), jnp.bfloat16),
        in_specs=vmem(8),
        out_specs=vmem(1)[0],
        scratch_shapes=[pltpu.VMEM((tok_rows, LANES), jnp.float32)] * 2,
        name="gated_rows",
    )(feats, halo, short_filter, log_decay, residue, driven, before, incoming)


def project_gathered(gated, residual, out_weight):
    columns = lax.all_to_all(out_weight, "tp", split_axis=1, concat_axis=0, tiled=True)
    weight = lax.all_gather(columns, "ctx", axis=0, tiled=True)
    rows = lax.all_gather(gated, "tp", axis=1, tiled=True)
    projected = jnp.dot(rows, weight, preferred_element_type=jnp.float32)
    return (residual.astype(jnp.float32) + projected).astype(jnp.bfloat16)


def cube_kernel(
    piece, flags, own_c, own_o, other_c, other_o, *refs
):
    weights, (theirs, mine, left) = refs[:-3], refs[-3:]
    tile = pl.program_id(0)
    half = pl.num_programs(0) // 2
    x, y, same = flags[1], flags[2], flags[3]
    rows = own_c.shape[0]

    @pl.when(tile == 0)
    def _():
        def fill(plane, token, source):
            for xr in range(2):
                for yr in range(2):
                    at = jnp.bitwise_xor(x, xr) * 2 + jnp.bitwise_xor(y, yr)
                    place = ((plane * 2 + xr) * 2 + yr) * piece
                    left[pl.ds(token * rows, rows), pl.ds(place, piece)] = source[
                        :, pl.ds(pl.multiple_of(at * piece, piece), piece)
                    ]

        @pl.when(same == 1)
        def _():
            fill(0, 0, own_c)
            fill(0, 1, own_o)
            fill(1, 0, other_c)
            fill(1, 1, other_o)

        @pl.when(same == 0)
        def _():
            fill(0, 0, other_c)
            fill(0, 1, other_o)
            fill(1, 0, own_c)
            fill(1, 1, own_o)

    right = jnp.concatenate([w[...] for w in weights], axis=0)
    total = jnp.dot(left[...], right, preferred_element_type=jnp.float32)

    @pl.when(tile < half)
    def _():
        theirs[...] = total.astype(jnp.bfloat16)

    @pl.when(tile >= half)
    def _():
        mine[...] = total


def cube_product(flags, gated, weights, piece, width, part):
    rows = gated[0].shape[0]
    tile = min(width, 256)
    half = width // tile

    def weight_map(chunked):
        per_core = half if chunked else weights[0][0].shape[1] // 2 // tile
        start = 0 if chunked else part * half

        def at(i, flags):
            core = jnp.where(i < half, 1 - flags[0], flags[0])
            return (0, core * per_core + start + lax.rem(i, half))

        return at

    whole = pl.BlockSpec(gated[0].shape, lambda i, flags: (0, 0))
    return pl.pallas_call(
        functools.partial(cube_kernel, piece),
        out_shape=(
            jax.ShapeDtypeStruct((2 * rows, width), jnp.bfloat16),
            jax.ShapeDtypeStruct((2 * rows, width), jnp.float32),
        ),
        grid_spec=pltpu.PrefetchScalarGridSpec(
            num_scalar_prefetch=1,
            grid=(2 * half,),
            in_specs=[whole] * 4
            + [pl.BlockSpec((w.shape[0], tile), weight_map(chunked)) for w, chunked in weights],
            out_specs=(
                pl.BlockSpec((2 * rows, tile), lambda i, flags: (0, jnp.minimum(i, half - 1))),
                pl.BlockSpec((2 * rows, tile), lambda i, flags: (0, jnp.maximum(i - half, 0))),
            ),
            scratch_shapes=[pltpu.VMEM((2 * rows, 8 * piece), jnp.bfloat16)],
        ),
        name="cube_product",
    )(flags, *gated, *[w for w, _ in weights])


def project_cube(gated, residual, out_weight, chunks):
    ctx, tp = lax.axis_size("ctx"), lax.axis_size("tp")
    c, t = lax.axis_index("ctx"), lax.axis_index("tp")
    core, y = t & 1, t >> 1
    x, zp, zh = c & 1, (c >> 1) & 1, c >> 2
    piece, columns = out_weight.shape
    channels = columns // tp
    width = channels // chunks

    sides = [out_weight[:, : 2 * channels], out_weight[:, 2 * channels :]]
    near = jnp.where(y == 0, sides[0], sides[1])
    give = jnp.where(y == 0, sides[1], sides[0])
    cuts = [piece * 3 // 4, piece]
    early = [near[lo:hi] for lo, hi in zip([0] + cuts, cuts)]
    near_z = [flip(w, "ctx", 4) for w in early]
    take = flip(give, "tp", 2)
    near_x = flip(near, "ctx", 1)

    def part_of(value, j):
        starts = [k * channels + j * width for k in range(2)]
        return jnp.concatenate([value[:, at : at + width] for at in starts], axis=1)

    take_z = [flip(part_of(take, j), "ctx", 4) for j in range(chunks)]
    take_x = flip(take, "ctx", 1)
    near_zx = [flip(w, "ctx", 1) for w in near_z]
    take_zx = [flip(take_z[j], "ctx", 1) for j in range(chunks)]

    def operands(arrays, chunked=False):
        return [(w, chunked) for w in arrays]

    weights = [
        operands([near, take, near_x, take_x])
        + operands(near_z)
        + operands([take_z[j]], True)
        + operands(near_zx)
        + operands([take_zx[j]], True)
        for j in range(chunks)
    ]

    mine = jnp.where(core == 0, gated[0], gated[1])
    sib = jnp.where(core == 0, gated[1], gated[0])
    stays = core == zp
    pairs_q, pairs_r = [], []
    for ci in range(ctx):
        for ti in range(tp):
            if (ti & 1) == ((ci >> 1) & 1):
                pairs_q.append((ci * tp + ti, ci * tp + (ti ^ 1)))
            else:
                pairs_q.append((ci * tp + ti, (ci ^ 2) * tp + ti))
                pairs_r.append((ci * tp + ti, (ci ^ 2) * tp + (ti ^ 1)))
    q = lax.ppermute(jnp.where(stays, sib, mine), ("ctx", "tp"), pairs_q)
    r = lax.ppermute(sib, ("ctx", "tp"), pairs_r)
    own_c = jnp.where(stays, mine, q)
    own_o = jnp.where(stays, q, r)
    other_c = flip(own_c, "tp", 2)
    other_o = flip(own_o, "tp", 2)
    flags = jnp.stack([core, x, y, (y == zh).astype(jnp.int32)]).astype(jnp.int32)

    rows = residual.shape[0]
    outs = []
    for j in range(chunks):
        theirs, ours = cube_product(
            flags, (own_c, own_o, other_c, other_o), weights[j], piece, width, j
        )
        total = ours + flip(theirs, "tp", 1).astype(jnp.float32)
        pair = flip(total[rows:].astype(jnp.bfloat16), "ctx", 2)
        base = residual[:, j * width : (j + 1) * width].astype(jnp.float32)
        outs.append((base + (total[:rows] + pair.astype(jnp.float32))).astype(jnp.bfloat16))
    return jnp.concatenate(outs, axis=1)


def on_device(features, short_filter, log_decay, residue, residual, out_weight):
    ctx, tp = lax.axis_size("ctx"), lax.axis_size("tp")
    piece = out_weight.shape[0]
    if cube_shaped(ctx, tp) and piece == LANES:
        gated = gated_blocks(features, short_filter, log_decay, residue, 2)
        return project_cube(gated, residual, out_weight, CHUNKS)
    gated = gated_blocks(features, short_filter, log_decay, residue, 1)[0]
    return project_gathered(gated, residual, out_weight)


def cube_shaped(ctx, tp):
    return tp == 4 and ctx == 2 * tp


def solution(mesh):
    return jax.shard_map(
        on_device,
        mesh=mesh,
        in_specs=(
            P("ctx", None, "tp"),
            P(None, None, "tp"),
            P(None, "tp"),
            P(None, "tp"),
            P("ctx", "tp"),
            P(("ctx", "tp"), None),
        ),
        out_specs=P("ctx", "tp"),
        check_vma=False,
    )
```

```python
import functools

import jax
import jax.numpy as jnp
from jax import lax
from jax.experimental import pallas as pl
from jax.experimental.pallas import tpu as pltpu
from jax.sharding import PartitionSpec as P


LANES = 128
CHUNKS = 2
UNROLL = 16
Z_CUT, X_CUT = 6, 4
SEGS = 8


def row(ref_value, n):
    return jnp.broadcast_to(ref_value[n : n + 1, :], (SEGS, ref_value.shape[1]))


def shifted(value, halo_row):
    lane_row = lax.broadcasted_iota(jnp.int32, value.shape, 0)
    return jnp.where(lane_row == 0, halo_row, pltpu.roll(value, 1, 0))


def history(tokens, halo, stream, lanes, seg_len, filter_len):
    rim = halo[stream, :, lanes].astype(jnp.float32)
    past = []
    for back in range(1, filter_len):
        last = tokens[pl.ds(seg_len - back, SEGS, stride=seg_len), :]
        past.append(shifted(last, rim[filter_len - 1 - back : filter_len - back, :]))
    return past


def taps_of(taps, stream, lanes, filter_len):
    values = taps[stream, :, lanes]
    return [row(values, j) for j in range(filter_len)]


def filter_step(now, past, taps):
    total = taps[0] * now
    for tap, old in zip(taps[1:], past):
        total = total + tap * old
    return total, [now] + past[:-1]


def scan_kernel(
    seg_len, feats, halo, taps, decay, driven, end, before, k_rows, v_rows
):
    modes, channels = decay.shape
    filter_len = taps.shape[1]
    seg = lax.broadcasted_iota(jnp.int32, (SEGS, LANES), 0)

    def one_group(group, _):
        lanes = pl.ds(pl.multiple_of(group * LANES, LANES), LANES)
        rate = decay[:, lanes]
        per_token = jnp.exp(-rate)
        step = [row(per_token, n) for n in range(modes)]
        k_rows[...] = feats[1, :, lanes].astype(jnp.float32)
        v_rows[...] = feats[2, :, lanes].astype(jnp.float32)
        k_taps = taps_of(taps, 1, lanes, filter_len)
        v_taps = taps_of(taps, 2, lanes, filter_len)

        def one_token(i, carry):
            states, k_past, v_past = carry
            at = pl.ds(i, SEGS, stride=seg_len)
            k, k_past = filter_step(k_rows[at, :], k_past, k_taps)
            v, v_past = filter_step(v_rows[at, :], v_past, v_taps)
            drive = k * v
            driven[i, :, lanes] = drive
            states = [a * s + drive for a, s in zip(step, states)]
            return states, k_past, v_past

        zero = jnp.zeros((SEGS, LANES), jnp.float32)
        states, _, _ = lax.fori_loop(
            0,
            seg_len,
            one_token,
            (
                [zero] * modes,
                history(k_rows, halo, 1, lanes, seg_len, filter_len),
                history(v_rows, halo, 2, lanes, seg_len, filter_len),
            ),
            unroll=UNROLL,
        )
        hop = 1
        while hop < SEGS:
            weight = jnp.exp(-rate * float(seg_len * hop))
            states = [
                s + row(weight, n) * jnp.where(seg >= hop, pltpu.roll(s, hop, 0), 0.0)
                for n, s in enumerate(states)
            ]
            hop *= 2
        for n, s in enumerate(states):
            end[n : n + 1, lanes] = s[SEGS - 1 :, :]
            before[n, :, lanes] = jnp.where(seg >= 1, pltpu.roll(s, 1, 0), 0.0)
        return 0

    lax.fori_loop(0, channels // LANES, one_group, 0)


def local_kernel(
    seg_len, feats, halo, taps, decay, residue, driven, before, gate, local, q_rows
):
    modes, channels = decay.shape
    filter_len = taps.shape[1]

    def one_group(group, _):
        lanes = pl.ds(pl.multiple_of(group * LANES, LANES), LANES)
        per_token = jnp.exp(-decay[:, lanes])
        weights = residue[:, lanes]
        q_rows[...] = feats[0, :, lanes].astype(jnp.float32)
        step = [row(per_token, n) for n in range(modes)]
        gain = [row(weights, n) for n in range(modes)]
        q_taps = taps_of(taps, 0, lanes, filter_len)

        def one_token(i, carry):
            states, q_past = carry
            at = pl.ds(i, SEGS, stride=seg_len)
            now, q_past = filter_step(q_rows[at, :], q_past, q_taps)
            gate[i, :, lanes] = now
            drive = driven[i, :, lanes]
            states = [a * s + drive for a, s in zip(step, states)]
            local[i, :, lanes] = tree_sum([r * s for r, s in zip(gain, states)])
            return states, q_past

        lax.fori_loop(
            0,
            seg_len,
            one_token,
            (
                [before[n, :, lanes] for n in range(modes)],
                history(q_rows, halo, 0, lanes, seg_len, filter_len),
            ),
            unroll=UNROLL,
        )
        return 0

    lax.fori_loop(0, channels // LANES, one_group, 0)


def tree_sum(terms):
    while len(terms) > 1:
        terms = [a + b for a, b in zip(terms[::2], terms[1::2])] + terms[len(terms) & ~1 :]
    return terms[0]


def output_kernel(seg_len, parts, flags, decay, residue, gate, local, incoming, *refs):
    outs, rows = refs[:parts], refs[parts]
    modes, channels = decay.shape
    seg = lax.broadcasted_iota(jnp.int32, (SEGS, LANES), 0).astype(jnp.float32)

    def one_group(group, _):
        lanes = pl.ds(pl.multiple_of(group * LANES, LANES), LANES)
        rate = decay[:, lanes]
        per_token = jnp.exp(-rate)
        entering = residue[:, lanes] * incoming[:, lanes]
        step = [row(per_token, n) for n in range(modes)]
        since = seg * float(seg_len) + 1.0
        terms = [jnp.exp(-row(rate, n) * since) * row(entering, n) for n in range(modes)]

        def one_token(i, terms):
            total = local[i, :, lanes] + tree_sum(terms)
            rows[pl.ds(i, SEGS, stride=seg_len), :] = gate[i, :, lanes] * total
            return [a * term for a, term in zip(step, terms)]

        lax.fori_loop(0, seg_len, one_token, terms, unroll=UNROLL)
        place = pl.ds(pl.multiple_of((group // parts) * LANES, LANES), LANES)
        value = rows[...].astype(jnp.bfloat16)
        turned = jnp.bitwise_xor(lax.rem(group, parts), flags[0] if parts > 1 else 0)
        for k in range(parts):

            @pl.when(turned == k)
            def _(k=k):
                outs[k][:, place] = value

        return 0

    lax.fori_loop(0, channels // LANES, one_group, 0)


def flip(value, axis, bit):
    count = lax.axis_size(axis)
    return lax.ppermute(value, axis, [(i, i ^ bit) for i in range(count)])


def entering_state(end, log_decay, tok_rows):
    place = lax.axis_index("ctx")
    count = lax.axis_size("ctx")
    prefix = jnp.zeros_like(end)
    total = end
    bit = 1
    while bit < count:
        other = flip(total, "ctx", bit)
        upper = (place & bit) != 0
        covered = (place & (bit - 1)).astype(jnp.float32) * float(tok_rows)
        prefix = prefix + jnp.where(upper, jnp.exp(-log_decay * covered) * other, 0.0)
        first = jnp.where(upper, other, total)
        second = jnp.where(upper, total, other)
        total = jnp.exp(-log_decay * float(tok_rows * bit)) * first + second
        bit *= 2
    return prefix


def in_vmem(kernel, out_shape, inputs, scratch, flops, flags=None):
    arrays = [pltpu.with_memory_space_constraint(a, pltpu.VMEM) for a in inputs]
    specs = [pl.BlockSpec(memory_space=pltpu.VMEM)] * len(arrays)
    if flags is not None:
        arrays, specs = [flags] + arrays, [pl.BlockSpec(memory_space=pltpu.SMEM)] + specs
    single = not isinstance(out_shape, tuple)
    return pl.pallas_call(
        kernel,
        out_shape=out_shape,
        in_specs=specs,
        out_specs=pl.BlockSpec(memory_space=pltpu.VMEM)
        if single
        else (pl.BlockSpec(memory_space=pltpu.VMEM),) * len(out_shape),
        scratch_shapes=scratch,
        compiler_params=pltpu.CompilerParams(vmem_limit_bytes=8 << 20),
        cost_estimate=pl.CostEstimate(flops=flops, bytes_accessed=flops // 200, transcendentals=0),
    )(*arrays)


def gated_blocks(features, short_filter, log_decay, residue, flags, parts):
    tok_rows, _, channels = features.shape
    filter_len = short_filter.shape[1]
    modes = log_decay.shape[0]
    seg_len = tok_rows // SEGS
    count = lax.axis_size("ctx")
    rim = lax.ppermute(
        features[tok_rows - (filter_len - 1) :],
        "ctx",
        [(i, i + 1) for i in range(count - 1)],
    )
    feats = jnp.transpose(features, (1, 0, 2))
    halo = jnp.transpose(rim, (1, 0, 2))
    tokens = pltpu.VMEM((seg_len, SEGS, channels), jnp.float32)
    states = pltpu.VMEM((modes, channels), jnp.float32)
    starts = pltpu.VMEM((modes, SEGS, channels), jnp.float32)
    lane_rows = pltpu.VMEM((tok_rows, LANES), jnp.float32)
    flops = 400 * tok_rows * channels * modes
    inputs = (feats, halo, short_filter, log_decay)
    driven, end, before = in_vmem(
        functools.partial(scan_kernel, seg_len),
        (tokens, states, starts),
        inputs,
        [lane_rows] * 2,
        flops,
    )
    incoming = entering_state(end, log_decay, tok_rows)
    gate, local = in_vmem(
        functools.partial(local_kernel, seg_len),
        (tokens, tokens),
        (*inputs, residue, driven, before),
        [lane_rows],
        flops,
    )
    out = pltpu.VMEM((tok_rows, channels // parts), jnp.bfloat16)
    return in_vmem(
        functools.partial(output_kernel, seg_len, parts),
        (out,) * parts,
        (log_decay, residue, gate, local, incoming),
        [lane_rows],
        flops,
        flags,
    )


def project_gathered(gated, residual, out_weight):
    columns = lax.all_to_all(out_weight, "tp", split_axis=1, concat_axis=0, tiled=True)
    weight = lax.all_gather(columns, "ctx", axis=0, tiled=True)
    rows = lax.all_gather(gated, "tp", axis=1, tiled=True)
    projected = jnp.dot(rows, weight, preferred_element_type=jnp.float32)
    return (residual.astype(jnp.float32) + projected).astype(jnp.bfloat16)


def fill_left(left, flags, piece, near_plane, far_plane):
    x, y = flags[1], flags[2]
    rows = near_plane[0].shape[0]
    for plane, sources in enumerate((near_plane, far_plane)):
        for token, source in enumerate(sources):
            for xr in range(2):
                for yr in range(2):
                    at = jnp.bitwise_xor(x, xr) * 2 + jnp.bitwise_xor(y, yr)
                    place = ((plane * 2 + xr) * 2 + yr) * piece
                    left[pl.ds(token * rows, rows), pl.ds(place, piece)] = source[
                        :, pl.ds(pl.multiple_of(at * piece, piece), piece)
                    ]


def cube_kernel(piece, chunked, part, flags, own_c, own_o, other_c, other_o, *refs):
    weights, (theirs, mine, left) = refs[:-3], refs[-3:]
    width = mine.shape[1]
    full = weights[0].shape[1] // 2
    tile = min(width, 256)
    own, other = (own_c, own_o), (other_c, other_o)

    @pl.when(flags[3] == 1)
    def _():
        fill_left(left, flags, piece, own, other)

    @pl.when(flags[3] == 0)
    def _():
        fill_left(left, flags, piece, other, own)

    for side, out in ((1 - flags[0], theirs), (flags[0], mine)):

        def one_tile(i, _, side=side, out=out):
            def columns(k):
                first = side * width if chunked[k] else side * full + part * width
                return pl.ds(pl.multiple_of(first + i * tile, tile), tile)

            right = jnp.concatenate([w[:, columns(k)] for k, w in enumerate(weights)], axis=0)
            total = jnp.dot(left[...], right, preferred_element_type=jnp.float32)
            out[:, pl.ds(pl.multiple_of(i * tile, tile), tile)] = total.astype(out.dtype)
            return 0

        lax.fori_loop(0, width // tile, one_tile, 0)


def cube_product(flags, gated, weights, piece, width, part):
    rows = 2 * gated[0].shape[0]
    depth = sum(w.shape[0] for w, _ in weights)
    return in_vmem(
        functools.partial(cube_kernel, piece, [chunked for _, chunked in weights], part),
        (pltpu.VMEM((rows, width), jnp.bfloat16), pltpu.VMEM((rows, width), jnp.float32)),
        (*gated, *[w for w, _ in weights]),
        [pltpu.VMEM((rows, depth), jnp.bfloat16)],
        4 * rows * width * depth,
        flags,
    )


def cube_place():
    c, t = lax.axis_index("ctx"), lax.axis_index("tp")
    core, y = t & 1, t >> 1
    x, zp, zh = c & 1, (c >> 1) & 1, c >> 2
    return core, y, x, zp, zh


def project_cube(mine, sib, flags, residual, out_weight, chunks):
    ctx, tp = lax.axis_size("ctx"), lax.axis_size("tp")
    core, y, _, zp, _ = cube_place()
    piece, columns = out_weight.shape
    channels = columns // tp
    width = channels // chunks

    sides = [out_weight[:, : 2 * channels], out_weight[:, 2 * channels :]]
    near = jnp.where(y == 0, sides[0], sides[1])
    give = jnp.where(y == 0, sides[1], sides[0])

    def cut_rows(value, cuts):
        return [value[lo:hi] for lo, hi in zip([0] + cuts, cuts + [piece])]

    near_z = [flip(w, "ctx", 4) for w in cut_rows(near, [piece * Z_CUT // 8])]
    near_x = [flip(w, "ctx", 1) for w in cut_rows(near, [piece * X_CUT // 8])]
    take = flip(give, "tp", 2)

    def part_of(value, j):
        starts = [k * channels + j * width for k in range(2)]
        return jnp.concatenate([value[:, at : at + width] for at in starts], axis=1)

    take_z = [flip(part_of(take, j), "ctx", 4) for j in range(chunks)]
    take_x = flip(take, "ctx", 1)
    near_zx = [flip(w, "ctx", 1) for w in near_z]
    take_zx = [flip(take_z[j], "ctx", 1) for j in range(chunks)]

    stays = core == zp
    pairs_1, pairs_2, pairs_3 = [], [], []
    for ci in range(ctx):
        for ti in range(tp):
            source = ci * tp + ti
            if (ti & 1) == ((ci >> 1) & 1):
                pairs_1.append((source, ci * tp + (ti ^ 1)))
            else:
                pairs_2.append((source, (ci ^ 2) * tp + ti))
                pairs_3.append((source, (ci ^ 2) * tp + (ti ^ 1)))

    def move(value, pairs):
        return lax.ppermute(value, ("ctx", "tp"), pairs)

    from_core = move(sib, pairs_1)
    from_z = move(mine, pairs_2)
    from_both = move(sib, pairs_3)
    own_c = jnp.where(stays, mine, from_core)
    own_o = jnp.where(stays, from_z, from_both)
    other_c = flip(own_c, "tp", 2)
    other_o = flip(own_o, "tp", 2)
    gated = (own_c, own_o, other_c, other_o)

    rows = residual.shape[0]
    outs = []
    for j in range(chunks):
        weights = [(w, False) for w in (near, take, *near_x, take_x, *near_z)]
        weights += [(take_z[j], True)] + [(w, False) for w in near_zx] + [(take_zx[j], True)]
        theirs, ours = cube_product(flags, gated, weights, piece, width, j)
        total = ours + flip(theirs, "tp", 1).astype(jnp.float32)
        pair = flip(total[rows:].astype(jnp.bfloat16), "ctx", 2)
        base = residual[:, j * width : (j + 1) * width].astype(jnp.float32)
        outs.append((base + (total[:rows] + pair.astype(jnp.float32))).astype(jnp.bfloat16))
    return jnp.concatenate(outs, axis=1)


def on_device(features, short_filter, log_decay, residue, residual, out_weight):
    ctx, tp = lax.axis_size("ctx"), lax.axis_size("tp")
    piece = out_weight.shape[0]
    if cube_shaped(ctx, tp) and piece == LANES:
        core, y, x, _, zh = cube_place()
        flags = jnp.stack([core, x, y, (y == zh).astype(jnp.int32)]).astype(jnp.int32)
        mine, sib = gated_blocks(features, short_filter, log_decay, residue, flags, 2)
        return project_cube(mine, sib, flags, residual, out_weight, CHUNKS)
    flags = jnp.zeros((1,), jnp.int32)
    (gated,) = gated_blocks(features, short_filter, log_decay, residue, flags, 1)
    return project_gathered(gated, residual, out_weight)


def cube_shaped(ctx, tp):
    return tp == 4 and ctx == 2 * tp


def solution(mesh):
    return jax.shard_map(
        on_device,
        mesh=mesh,
        in_specs=(
            P("ctx", None, "tp"),
            P(None, None, "tp"),
            P(None, "tp"),
            P(None, "tp"),
            P("ctx", "tp"),
            P(("ctx", "tp"), None),
        ),
        out_specs=P("ctx", "tp"),
        check_vma=False,
    )
```

```python
import functools

import jax
import jax.numpy as jnp
from jax import lax
from jax.experimental import pallas as pl
from jax.experimental.pallas import tpu as pltpu
from jax.sharding import PartitionSpec as P


LANES = 128
CHUNKS = 2
UNROLL = 16
CUTS = (3,)
CORE_FIRST, PART_FIRST, ONE_PART = range(3)
SEGS = 8


def row(ref_value, n):
    return jnp.broadcast_to(ref_value[n : n + 1, :], (SEGS, ref_value.shape[1]))


def shifted(value, halo_row):
    lane_row = lax.broadcasted_iota(jnp.int32, value.shape, 0)
    return jnp.where(lane_row == 0, halo_row, pltpu.roll(value, 1, 0))


def history(tokens, halo, stream, lanes, seg_len, filter_len):
    rim = halo[stream, :, lanes].astype(jnp.float32)
    past = []
    for back in range(1, filter_len):
        last = tokens[pl.ds(seg_len - back, SEGS, stride=seg_len), :]
        past.append(shifted(last, rim[filter_len - 1 - back : filter_len - back, :]))
    return past


def taps_of(taps, stream, lanes, filter_len):
    values = taps[stream, :, lanes]
    return [row(values, j) for j in range(filter_len)]


def filter_step(now, past, taps):
    total = taps[0] * now
    for tap, old in zip(taps[1:], past):
        total = total + tap * old
    return total, [now] + past[:-1]


def scan_kernel(
    seg_len, feats, halo, taps, decay, end, before, k_rows, v_rows
):
    modes, channels = decay.shape
    filter_len = taps.shape[1]
    seg = lax.broadcasted_iota(jnp.int32, (SEGS, LANES), 0)

    def one_group(group, _):
        lanes = pl.ds(pl.multiple_of(group * LANES, LANES), LANES)
        rate = decay[:, lanes]
        per_token = jnp.exp(-rate)
        step = [row(per_token, n) for n in range(modes)]
        k_rows[...] = feats[1, :, lanes].astype(jnp.float32)
        v_rows[...] = feats[2, :, lanes].astype(jnp.float32)
        k_taps = taps_of(taps, 1, lanes, filter_len)
        v_taps = taps_of(taps, 2, lanes, filter_len)

        def one_token(i, carry):
            states, k_past, v_past = carry
            at = pl.ds(i, SEGS, stride=seg_len)
            k, k_past = filter_step(k_rows[at, :], k_past, k_taps)
            v, v_past = filter_step(v_rows[at, :], v_past, v_taps)
            drive = k * v
            states = [a * s + drive for a, s in zip(step, states)]
            return states, k_past, v_past

        zero = jnp.zeros((SEGS, LANES), jnp.float32)
        states, _, _ = lax.fori_loop(
            0,
            seg_len,
            one_token,
            (
                [zero] * modes,
                history(k_rows, halo, 1, lanes, seg_len, filter_len),
                history(v_rows, halo, 2, lanes, seg_len, filter_len),
            ),
            unroll=UNROLL,
        )
        hop = 1
        while hop < SEGS:
            weight = jnp.exp(-rate * float(seg_len * hop))
            states = [
                s + row(weight, n) * jnp.where(seg >= hop, pltpu.roll(s, hop, 0), 0.0)
                for n, s in enumerate(states)
            ]
            hop *= 2
        for n, s in enumerate(states):
            end[n : n + 1, lanes] = s[SEGS - 1 :, :]
            before[n, :, lanes] = jnp.where(seg >= 1, pltpu.roll(s, 1, 0), 0.0)
        return 0

    lax.fori_loop(0, channels // LANES, one_group, 0)


def local_kernel(
    seg_len, feats, halo, taps, decay, residue, before, gate, local, q_rows, k_rows, v_rows
):
    modes, channels = decay.shape
    filter_len = taps.shape[1]

    def one_group(group, _):
        lanes = pl.ds(pl.multiple_of(group * LANES, LANES), LANES)
        per_token = jnp.exp(-decay[:, lanes])
        weights = residue[:, lanes]
        q_rows[...] = feats[0, :, lanes].astype(jnp.float32)
        step = [row(per_token, n) for n in range(modes)]
        gain = [row(weights, n) for n in range(modes)]
        k_rows[...] = feats[1, :, lanes].astype(jnp.float32)
        v_rows[...] = feats[2, :, lanes].astype(jnp.float32)
        q_taps = taps_of(taps, 0, lanes, filter_len)
        k_taps = taps_of(taps, 1, lanes, filter_len)
        v_taps = taps_of(taps, 2, lanes, filter_len)

        def one_token(i, carry):
            states, q_past, k_past, v_past = carry
            at = pl.ds(i, SEGS, stride=seg_len)
            now, q_past = filter_step(q_rows[at, :], q_past, q_taps)
            k, k_past = filter_step(k_rows[at, :], k_past, k_taps)
            v, v_past = filter_step(v_rows[at, :], v_past, v_taps)
            gate[i, :, lanes] = now
            drive = k * v
            states = [a * s + drive for a, s in zip(step, states)]
            local[i, :, lanes] = tree_sum([r * s for r, s in zip(gain, states)])
            return states, q_past, k_past, v_past

        lax.fori_loop(
            0,
            seg_len,
            one_token,
            (
                [before[n, :, lanes] for n in range(modes)],
                history(q_rows, halo, 0, lanes, seg_len, filter_len),
                history(k_rows, halo, 1, lanes, seg_len, filter_len),
                history(v_rows, halo, 2, lanes, seg_len, filter_len),
            ),
            unroll=UNROLL,
        )
        return 0

    lax.fori_loop(0, channels // LANES, one_group, 0)


def tree_sum(terms):
    while len(terms) > 1:
        terms = [a + b for a, b in zip(terms[::2], terms[1::2])] + terms[len(terms) & ~1 :]
    return terms[0]


def output_kernel(seg_len, parts, flags, decay, residue, gate, local, incoming, *refs):
    outs, rows = refs[:parts], refs[parts]
    modes, channels = decay.shape
    seg = lax.broadcasted_iota(jnp.int32, (SEGS, LANES), 0).astype(jnp.float32)

    def one_group(group, _):
        lanes = pl.ds(pl.multiple_of(group * LANES, LANES), LANES)
        rate = decay[:, lanes]
        per_token = jnp.exp(-rate)
        entering = residue[:, lanes] * incoming[:, lanes]
        step = [row(per_token, n) for n in range(modes)]
        since = seg * float(seg_len) + 1.0
        terms = [jnp.exp(-row(rate, n) * since) * row(entering, n) for n in range(modes)]

        def one_token(i, terms):
            total = local[i, :, lanes] + tree_sum(terms)
            rows[pl.ds(i, SEGS, stride=seg_len), :] = gate[i, :, lanes] * total
            return [a * term for a, term in zip(step, terms)]

        lax.fori_loop(0, seg_len, one_token, terms, unroll=UNROLL)
        place = pl.ds(pl.multiple_of((group // parts) * LANES, LANES), LANES)
        value = rows[...].astype(jnp.bfloat16)
        turned = jnp.bitwise_xor(lax.rem(group, parts), flags[0] if parts > 1 else 0)
        for k in range(parts):

            @pl.when(turned == k)
            def _(k=k):
                outs[k][:, place] = value

        return 0

    lax.fori_loop(0, channels // LANES, one_group, 0)


def flip(value, axis, bit):
    count = lax.axis_size(axis)
    return lax.ppermute(value, axis, [(i, i ^ bit) for i in range(count)])


def entering_state(end, log_decay, tok_rows):
    place = lax.axis_index("ctx")
    count = lax.axis_size("ctx")
    prefix = jnp.zeros_like(end)
    total = end
    bit = 1
    while bit < count:
        other = flip(total, "ctx", bit)
        upper = (place & bit) != 0
        covered = (place & (bit - 1)).astype(jnp.float32) * float(tok_rows)
        prefix = prefix + jnp.where(upper, jnp.exp(-log_decay * covered) * other, 0.0)
        first = jnp.where(upper, other, total)
        second = jnp.where(upper, total, other)
        total = jnp.exp(-log_decay * float(tok_rows * bit)) * first + second
        bit *= 2
    return prefix


def in_vmem(kernel, out_shape, inputs, scratch, flops, flags=None):
    arrays = [pltpu.with_memory_space_constraint(a, pltpu.VMEM) for a in inputs]
    specs = [pl.BlockSpec(memory_space=pltpu.VMEM)] * len(arrays)
    if flags is not None:
        arrays, specs = [flags] + arrays, [pl.BlockSpec(memory_space=pltpu.SMEM)] + specs
    single = not isinstance(out_shape, tuple)
    return pl.pallas_call(
        kernel,
        out_shape=out_shape,
        in_specs=specs,
        out_specs=pl.BlockSpec(memory_space=pltpu.VMEM)
        if single
        else (pl.BlockSpec(memory_space=pltpu.VMEM),) * len(out_shape),
        scratch_shapes=scratch,
        compiler_params=pltpu.CompilerParams(vmem_limit_bytes=8 << 20),
        cost_estimate=pl.CostEstimate(flops=flops, bytes_accessed=flops // 200, transcendentals=0),
    )(*arrays)


def gated_blocks(features, short_filter, log_decay, residue, flags, parts):
    tok_rows, _, channels = features.shape
    filter_len = short_filter.shape[1]
    modes = log_decay.shape[0]
    seg_len = tok_rows // SEGS
    count = lax.axis_size("ctx")
    rim = lax.ppermute(
        features[tok_rows - (filter_len - 1) :],
        "ctx",
        [(i, i + 1) for i in range(count - 1)],
    )
    feats = jnp.transpose(features, (1, 0, 2))
    halo = jnp.transpose(rim, (1, 0, 2))
    tokens = pltpu.VMEM((seg_len, SEGS, channels), jnp.float32)
    states = pltpu.VMEM((modes, channels), jnp.float32)
    starts = pltpu.VMEM((modes, SEGS, channels), jnp.float32)
    lane_rows = pltpu.VMEM((tok_rows, LANES), jnp.float32)
    flops = 400 * tok_rows * channels * modes
    inputs = (feats, halo, short_filter, log_decay)
    end, before = in_vmem(
        functools.partial(scan_kernel, seg_len), (states, starts), inputs, [lane_rows] * 2, flops
    )
    incoming = entering_state(end, log_decay, tok_rows)
    gate, local = in_vmem(
        functools.partial(local_kernel, seg_len),
        (tokens, tokens),
        (*inputs, residue, before),
        [lane_rows] * 3,
        flops,
    )
    out = pltpu.VMEM((tok_rows, channels // parts), jnp.bfloat16)
    return in_vmem(
        functools.partial(output_kernel, seg_len, parts),
        (out,) * parts,
        (log_decay, residue, gate, local, incoming),
        [lane_rows],
        flops,
        flags,
    )


def project_gathered(gated, residual, out_weight):
    columns = lax.all_to_all(out_weight, "tp", split_axis=1, concat_axis=0, tiled=True)
    weight = lax.all_gather(columns, "ctx", axis=0, tiled=True)
    rows = lax.all_gather(gated, "tp", axis=1, tiled=True)
    projected = jnp.dot(rows, weight, preferred_element_type=jnp.float32)
    return (residual.astype(jnp.float32) + projected).astype(jnp.bfloat16)


def fill_left(left, flags, piece, near_plane, far_plane):
    x, y = flags[1], flags[2]
    rows = near_plane[0].shape[0]
    for plane, sources in enumerate((near_plane, far_plane)):
        for token, source in enumerate(sources):
            for xr in range(2):
                for yr in range(2):
                    at = jnp.bitwise_xor(x, xr) * 2 + jnp.bitwise_xor(y, yr)
                    place = ((plane * 2 + xr) * 2 + yr) * piece
                    left[pl.ds(token * rows, rows), pl.ds(place, piece)] = source[
                        :, pl.ds(pl.multiple_of(at * piece, piece), piece)
                    ]


def cube_kernel(piece, orders, part, flags, own_c, own_o, other_c, other_o, *refs):
    weights, (theirs, mine, left) = refs[:-3], refs[-3:]
    width = mine.shape[1]
    full = weights[0].shape[1] // 2
    tile = min(width, 256)
    own, other = (own_c, own_o), (other_c, other_o)

    @pl.when(flags[3] == 1)
    def _():
        fill_left(left, flags, piece, own, other)

    @pl.when(flags[3] == 0)
    def _():
        fill_left(left, flags, piece, other, own)

    for side, out in ((1 - flags[0], theirs), (flags[0], mine)):

        def one_tile(i, _, side=side, out=out):
            def columns(k):
                first = {
                    CORE_FIRST: side * full + part * width,
                    PART_FIRST: (2 * part + side) * width,
                    ONE_PART: side * width,
                }[orders[k]]
                return pl.ds(pl.multiple_of(first + i * tile, tile), tile)

            right = jnp.concatenate([w[:, columns(k)] for k, w in enumerate(weights)], axis=0)
            total = jnp.dot(left[...], right, preferred_element_type=jnp.float32)
            out[:, pl.ds(pl.multiple_of(i * tile, tile), tile)] = total.astype(out.dtype)
            return 0

        lax.fori_loop(0, width // tile, one_tile, 0)


def cube_product(flags, gated, weights, piece, width, part):
    rows = 2 * gated[0].shape[0]
    depth = sum(w.shape[0] for w, _ in weights)
    return in_vmem(
        functools.partial(cube_kernel, piece, [order for _, order in weights], part),
        (pltpu.VMEM((rows, width), jnp.bfloat16), pltpu.VMEM((rows, width), jnp.float32)),
        (*gated, *[w for w, _ in weights]),
        [pltpu.VMEM((rows, depth), jnp.bfloat16)],
        4 * rows * width * depth,
        flags,
    )


def cube_place():
    c, t = lax.axis_index("ctx"), lax.axis_index("tp")
    core, y = t & 1, t >> 1
    x, zp, zh = c & 1, (c >> 1) & 1, c >> 2
    return core, y, x, zp, zh


def project_cube(mine, sib, flags, residual, out_weight, chunks):
    ctx, tp = lax.axis_size("ctx"), lax.axis_size("tp")
    core, y, _, zp, _ = cube_place()
    piece, columns = out_weight.shape
    channels = columns // tp
    width = channels // chunks

    sides = [out_weight[:, : 2 * channels], out_weight[:, 2 * channels :]]
    cuts = [0] + [piece * k // 8 for k in CUTS] + [piece]
    near = [
        jnp.where(y == 0, sides[0][lo:hi], sides[1][lo:hi]) for lo, hi in zip(cuts, cuts[1:])
    ]

    def parts_first(side):
        starts = [k * channels + j * width for j in range(chunks) for k in range(2)]
        return jnp.concatenate([side[:, at : at + width] for at in starts], axis=1)

    give = jnp.where(y == 0, parts_first(sides[1]), parts_first(sides[0]))
    near_z = [flip(w, "ctx", 4) for w in near]
    take = flip(give, "tp", 2)
    near_x = [flip(w, "ctx", 1) for w in near]
    take_z = [flip(take[:, 2 * j * width : 2 * (j + 1) * width], "ctx", 4) for j in range(chunks)]
    take_x = flip(take, "ctx", 1)
    near_zx = [flip(w, "ctx", 1) for w in near_z]
    take_zx = [flip(take_z[j], "ctx", 1) for j in range(chunks)]

    stays = core == zp
    pairs_1, pairs_2, pairs_3 = [], [], []
    for ci in range(ctx):
        for ti in range(tp):
            source = ci * tp + ti
            if (ti & 1) == ((ci >> 1) & 1):
                pairs_1.append((source, ci * tp + (ti ^ 1)))
            else:
                pairs_2.append((source, (ci ^ 2) * tp + ti))
                pairs_3.append((source, (ci ^ 2) * tp + (ti ^ 1)))

    def move(value, pairs):
        return lax.ppermute(value, ("ctx", "tp"), pairs)

    from_core = move(sib, pairs_1)
    from_z = move(mine, pairs_2)
    from_both = move(sib, pairs_3)
    own_c = jnp.where(stays, mine, from_core)
    own_o = jnp.where(stays, from_z, from_both)
    other_c = flip(own_c, "tp", 2)
    other_o = flip(own_o, "tp", 2)
    gated = (own_c, own_o, other_c, other_o)

    rows = residual.shape[0]
    outs = []
    for j in range(chunks):
        weights = [(w, CORE_FIRST) for w in near] + [(take, PART_FIRST)]
        weights += [(w, CORE_FIRST) for w in near_x] + [(take_x, PART_FIRST)]
        weights += [(w, CORE_FIRST) for w in near_z] + [(take_z[j], ONE_PART)]
        weights += [(w, CORE_FIRST) for w in near_zx] + [(take_zx[j], ONE_PART)]
        theirs, ours = cube_product(flags, gated, weights, piece, width, j)
        total = ours + flip(theirs, "tp", 1).astype(jnp.float32)
        pair = flip(total[rows:].astype(jnp.bfloat16), "ctx", 2)
        base = residual[:, j * width : (j + 1) * width].astype(jnp.float32)
        outs.append((base + (total[:rows] + pair.astype(jnp.float32))).astype(jnp.bfloat16))
    return jnp.concatenate(outs, axis=1)


def on_device(features, short_filter, log_decay, residue, residual, out_weight):
    ctx, tp = lax.axis_size("ctx"), lax.axis_size("tp")
    piece = out_weight.shape[0]
    if cube_shaped(ctx, tp) and piece == LANES:
        core, y, x, _, zh = cube_place()
        flags = jnp.stack([core, x, y, (y == zh).astype(jnp.int32)]).astype(jnp.int32)
        mine, sib = gated_blocks(features, short_filter, log_decay, residue, flags, 2)
        return project_cube(mine, sib, flags, residual, out_weight, CHUNKS)
    flags = jnp.zeros((1,), jnp.int32)
    (gated,) = gated_blocks(features, short_filter, log_decay, residue, flags, 1)
    return project_gathered(gated, residual, out_weight)


def cube_shaped(ctx, tp):
    return tp == 4 and ctx == 2 * tp


def solution(mesh):
    return jax.shard_map(
        on_device,
        mesh=mesh,
        in_specs=(
            P("ctx", None, "tp"),
            P(None, None, "tp"),
            P(None, "tp"),
            P(None, "tp"),
            P("ctx", "tp"),
            P(("ctx", "tp"), None),
        ),
        out_specs=P("ctx", "tp"),
        check_vma=False,
    )
```

```python
import functools

import jax
import jax.numpy as jnp
from jax import lax
from jax.experimental import pallas as pl
from jax.experimental.pallas import tpu as pltpu
from jax.sharding import PartitionSpec as P


LANES = 128
CHUNKS = 2
UNROLL = 16
CUTS = (3,)
CORE_FIRST, PART_FIRST, ONE_PART = range(3)
SEGS = 8


def row(ref_value, n):
    return jnp.broadcast_to(ref_value[n : n + 1, :], (SEGS, ref_value.shape[1]))


def shifted(value, halo_row):
    lane_row = lax.broadcasted_iota(jnp.int32, value.shape, 0)
    return jnp.where(lane_row == 0, halo_row, pltpu.roll(value, 1, 0))


def history(tokens, halo, stream, lanes, seg_len, filter_len):
    rim = halo[stream, :, lanes].astype(jnp.float32)
    past = []
    for back in range(1, filter_len):
        last = tokens[pl.ds(seg_len - back, SEGS, stride=seg_len), :]
        past.append(shifted(last, rim[filter_len - 1 - back : filter_len - back, :]))
    return past


def taps_of(taps, stream, lanes, filter_len):
    values = taps[stream, :, lanes]
    return [row(values, j) for j in range(filter_len)]


def filter_step(now, past, taps):
    total = taps[0] * now
    for tap, old in zip(taps[1:], past):
        total = total + tap * old
    return total, [now] + past[:-1]


def scan_kernel(
    seg_len, feats, halo, taps, decay, end, before, k_rows, v_rows
):
    modes, channels = decay.shape
    filter_len = taps.shape[1]
    seg = lax.broadcasted_iota(jnp.int32, (SEGS, LANES), 0)

    def one_group(group, _):
        lanes = pl.ds(pl.multiple_of(group * LANES, LANES), LANES)
        rate = decay[:, lanes]
        per_token = jnp.exp(-rate)
        step = [row(per_token, n) for n in range(modes)]
        k_rows[...] = feats[1, :, lanes].astype(jnp.float32)
        v_rows[...] = feats[2, :, lanes].astype(jnp.float32)
        k_taps = taps_of(taps, 1, lanes, filter_len)
        v_taps = taps_of(taps, 2, lanes, filter_len)

        def one_token(i, carry):
            states, k_past, v_past = carry
            at = pl.ds(i, SEGS, stride=seg_len)
            k, k_past = filter_step(k_rows[at, :], k_past, k_taps)
            v, v_past = filter_step(v_rows[at, :], v_past, v_taps)
            drive = k * v
            states = [a * s + drive for a, s in zip(step, states)]
            return states, k_past, v_past

        zero = jnp.zeros((SEGS, LANES), jnp.float32)
        states, _, _ = lax.fori_loop(
            0,
            seg_len,
            one_token,
            (
                [zero] * modes,
                history(k_rows, halo, 1, lanes, seg_len, filter_len),
                history(v_rows, halo, 2, lanes, seg_len, filter_len),
            ),
            unroll=UNROLL,
        )
        hop = 1
        while hop < SEGS:
            weight = jnp.exp(-rate * float(seg_len * hop))
            states = [
                s + row(weight, n) * jnp.where(seg >= hop, pltpu.roll(s, hop, 0), 0.0)
                for n, s in enumerate(states)
            ]
            hop *= 2
        for n, s in enumerate(states):
            end[n : n + 1, lanes] = s[SEGS - 1 :, :]
            before[n, :, lanes] = jnp.where(seg >= 1, pltpu.roll(s, 1, 0), 0.0)
        return 0

    lax.fori_loop(0, channels // LANES, one_group, 0)


def local_kernel(
    seg_len, feats, halo, taps, decay, residue, before, gate, local, q_rows, k_rows, v_rows
):
    modes, channels = decay.shape
    filter_len = taps.shape[1]

    def one_group(group, _):
        lanes = pl.ds(pl.multiple_of(group * LANES, LANES), LANES)
        per_token = jnp.exp(-decay[:, lanes])
        weights = residue[:, lanes]
        q_rows[...] = feats[0, :, lanes].astype(jnp.float32)
        step = [row(per_token, n) for n in range(modes)]
        gain = [row(weights, n) for n in range(modes)]
        k_rows[...] = feats[1, :, lanes].astype(jnp.float32)
        v_rows[...] = feats[2, :, lanes].astype(jnp.float32)
        q_taps = taps_of(taps, 0, lanes, filter_len)
        k_taps = taps_of(taps, 1, lanes, filter_len)
        v_taps = taps_of(taps, 2, lanes, filter_len)

        def one_token(i, carry):
            states, q_past, k_past, v_past = carry
            at = pl.ds(i, SEGS, stride=seg_len)
            now, q_past = filter_step(q_rows[at, :], q_past, q_taps)
            k, k_past = filter_step(k_rows[at, :], k_past, k_taps)
            v, v_past = filter_step(v_rows[at, :], v_past, v_taps)
            gate[i, :, lanes] = now
            drive = k * v
            states = [a * s + drive for a, s in zip(step, states)]
            local[i, :, lanes] = tree_sum([r * s for r, s in zip(gain, states)])
            return states, q_past, k_past, v_past

        lax.fori_loop(
            0,
            seg_len,
            one_token,
            (
                [before[n, :, lanes] for n in range(modes)],
                history(q_rows, halo, 0, lanes, seg_len, filter_len),
                history(k_rows, halo, 1, lanes, seg_len, filter_len),
                history(v_rows, halo, 2, lanes, seg_len, filter_len),
            ),
            unroll=UNROLL,
        )
        return 0

    lax.fori_loop(0, channels // LANES, one_group, 0)


def tree_sum(terms):
    while len(terms) > 1:
        terms = [a + b for a, b in zip(terms[::2], terms[1::2])] + terms[len(terms) & ~1 :]
    return terms[0]


def output_kernel(seg_len, parts, flags, decay, residue, gate, local, incoming, *refs):
    outs, rows = refs[:parts], refs[parts]
    modes, channels = decay.shape
    seg = lax.broadcasted_iota(jnp.int32, (SEGS, LANES), 0).astype(jnp.float32)

    def one_group(group, _):
        lanes = pl.ds(pl.multiple_of(group * LANES, LANES), LANES)
        rate = decay[:, lanes]
        per_token = jnp.exp(-rate)
        entering = residue[:, lanes] * incoming[:, lanes]
        step = [row(per_token, n) for n in range(modes)]
        since = seg * float(seg_len) + 1.0
        terms = [jnp.exp(-row(rate, n) * since) * row(entering, n) for n in range(modes)]

        def one_token(i, terms):
            total = local[i, :, lanes] + tree_sum(terms)
            rows[pl.ds(i, SEGS, stride=seg_len), :] = gate[i, :, lanes] * total
            return [a * term for a, term in zip(step, terms)]

        lax.fori_loop(0, seg_len, one_token, terms, unroll=UNROLL)
        place = pl.ds(pl.multiple_of((group // parts) * LANES, LANES), LANES)
        value = rows[...].astype(jnp.bfloat16)
        turned = jnp.bitwise_xor(lax.rem(group, parts), flags[4] if parts > 1 else 0)
        for k in range(parts):

            @pl.when(turned == k)
            def _(k=k):
                outs[k][:, place] = value

        return 0

    lax.fori_loop(0, channels // LANES, one_group, 0)


def flip(value, axis, bit):
    count = lax.axis_size(axis)
    return lax.ppermute(value, axis, [(i, i ^ bit) for i in range(count)])


def entering_state(end, log_decay, tok_rows):
    place = lax.axis_index("ctx")
    count = lax.axis_size("ctx")
    decay_over = lambda tokens: jnp.exp(-log_decay * tokens)
    prefix = jnp.zeros_like(end)
    total = end
    bit = 2
    while bit < count:
        other = flip(total, "ctx", bit)
        upper = (place & bit) != 0
        covered = (place & (bit - 2)).astype(jnp.float32) * float(tok_rows)
        prefix = prefix + jnp.where(upper, decay_over(covered) * other, 0.0)
        first = jnp.where(upper, other, total)
        second = jnp.where(upper, total, other)
        total = decay_over(float(tok_rows * bit)) * first + second
        bit *= 2
    even = (place & 1) == 0
    message = jnp.where(even, decay_over(float(2 * tok_rows)) * prefix + end, prefix)
    other = flip(message, "ctx", 1)
    return decay_over(float(tok_rows)) * prefix + other


def in_vmem(kernel, out_shape, inputs, scratch, flops, flags=None):
    arrays = [pltpu.with_memory_space_constraint(a, pltpu.VMEM) for a in inputs]
    specs = [pl.BlockSpec(memory_space=pltpu.VMEM)] * len(arrays)
    if flags is not None:
        arrays, specs = [flags] + arrays, [pl.BlockSpec(memory_space=pltpu.SMEM)] + specs
    single = not isinstance(out_shape, tuple)
    return pl.pallas_call(
        kernel,
        out_shape=out_shape,
        in_specs=specs,
        out_specs=pl.BlockSpec(memory_space=pltpu.VMEM)
        if single
        else (pl.BlockSpec(memory_space=pltpu.VMEM),) * len(out_shape),
        scratch_shapes=scratch,
        compiler_params=pltpu.CompilerParams(vmem_limit_bytes=8 << 20),
        cost_estimate=pl.CostEstimate(flops=flops, bytes_accessed=flops // 200, transcendentals=0),
    )(*arrays)


def gated_blocks(features, short_filter, log_decay, residue, flags, parts):
    tok_rows, _, channels = features.shape
    filter_len = short_filter.shape[1]
    modes = log_decay.shape[0]
    seg_len = tok_rows // SEGS
    count = lax.axis_size("ctx")
    rim = lax.ppermute(
        features[tok_rows - (filter_len - 1) :],
        "ctx",
        [(i, i + 1) for i in range(count - 1)],
    )
    feats = jnp.transpose(features, (1, 0, 2))
    halo = jnp.transpose(rim, (1, 0, 2))
    tokens = pltpu.VMEM((seg_len, SEGS, channels), jnp.float32)
    states = pltpu.VMEM((modes, channels), jnp.float32)
    starts = pltpu.VMEM((modes, SEGS, channels), jnp.float32)
    lane_rows = pltpu.VMEM((tok_rows, LANES), jnp.float32)
    flops = 400 * tok_rows * channels * modes
    inputs = (feats, halo, short_filter, log_decay)
    end, before = in_vmem(
        functools.partial(scan_kernel, seg_len), (states, starts), inputs, [lane_rows] * 2, flops
    )
    incoming = entering_state(end, log_decay, tok_rows)
    gate, local = in_vmem(
        functools.partial(local_kernel, seg_len),
        (tokens, tokens),
        (*inputs, residue, before),
        [lane_rows] * 3,
        flops,
    )
    out = pltpu.VMEM((tok_rows, channels // parts), jnp.bfloat16)
    return in_vmem(
        functools.partial(output_kernel, seg_len, parts),
        (out,) * parts,
        (log_decay, residue, gate, local, incoming),
        [lane_rows],
        flops,
        flags,
    )


def project_gathered(gated, residual, out_weight):
    columns = lax.all_to_all(out_weight, "tp", split_axis=1, concat_axis=0, tiled=True)
    weight = lax.all_gather(columns, "ctx", axis=0, tiled=True)
    rows = lax.all_gather(gated, "tp", axis=1, tiled=True)
    projected = jnp.dot(rows, weight, preferred_element_type=jnp.float32)
    return (residual.astype(jnp.float32) + projected).astype(jnp.bfloat16)


def fill_left(left, flags, piece, near_plane, far_plane):
    x, y = flags[1], flags[2]
    rows = near_plane[0].shape[0]
    for plane, sources in enumerate((near_plane, far_plane)):
        for token, source in enumerate(sources):
            for xr in range(2):
                for yr in range(2):
                    at = jnp.bitwise_xor(x, xr) * 2 + jnp.bitwise_xor(y, yr)
                    place = ((plane * 2 + xr) * 2 + yr) * piece
                    left[pl.ds(token * rows, rows), pl.ds(place, piece)] = source[
                        :, pl.ds(pl.multiple_of(at * piece, piece), piece)
                    ]


def cube_kernel(piece, orders, part, flags, kept, from_q, from_r, from_1, from_2, *refs):
    weights, (theirs, mine, left) = refs[:-3], refs[-3:]
    width = mine.shape[1]
    full = weights[0].shape[1] // 2
    tile = min(width, 256)

    for stays, own, other in (
        (1, (kept, from_q), (from_2, from_1)),
        (0, (from_q, from_r), (from_1, from_2)),
    ):
        for same, near_plane, far_plane in ((1, own, other), (0, other, own)):

            @pl.when(jnp.logical_and(flags[3] == same, flags[5] == stays))
            def _(near_plane=near_plane, far_plane=far_plane):
                fill_left(left, flags, piece, near_plane, far_plane)

    for side, out in ((1 - flags[0], theirs), (flags[0], mine)):

        def one_tile(i, _, side=side, out=out):
            def columns(k):
                first = {
                    CORE_FIRST: side * full + part * width,
                    PART_FIRST: (2 * part + side) * width,
                    ONE_PART: side * width,
                }[orders[k]]
                return pl.ds(pl.multiple_of(first + i * tile, tile), tile)

            right = jnp.concatenate([w[:, columns(k)] for k, w in enumerate(weights)], axis=0)
            total = jnp.dot(left[...], right, preferred_element_type=jnp.float32)
            out[:, pl.ds(pl.multiple_of(i * tile, tile), tile)] = total.astype(out.dtype)
            return 0

        lax.fori_loop(0, width // tile, one_tile, 0)


def cube_product(flags, gated, weights, piece, width, part):
    rows = 2 * gated[0].shape[0]
    depth = sum(w.shape[0] for w, _ in weights)
    return in_vmem(
        functools.partial(cube_kernel, piece, [order for _, order in weights], part),
        (pltpu.VMEM((rows, width), jnp.bfloat16), pltpu.VMEM((rows, width), jnp.float32)),
        (*gated, *[w for w, _ in weights]),
        [pltpu.VMEM((rows, depth), jnp.bfloat16)],
        4 * rows * width * depth,
        flags,
    )


def cube_place():
    c, t = lax.axis_index("ctx"), lax.axis_index("tp")
    core, y = t & 1, t >> 1
    x, zp, zh = c & 1, (c >> 1) & 1, c >> 2
    return core, y, x, zp, zh


def project_cube(leaves, turns, flags, residual, out_weight, chunks):
    ctx, tp = lax.axis_size("ctx"), lax.axis_size("tp")
    _, y, _, _, _ = cube_place()
    piece, columns = out_weight.shape
    channels = columns // tp
    width = channels // chunks

    sides = [out_weight[:, : 2 * channels], out_weight[:, 2 * channels :]]
    cuts = [0] + [piece * k // 8 for k in CUTS] + [piece]
    near = [
        jnp.where(y == 0, sides[0][lo:hi], sides[1][lo:hi]) for lo, hi in zip(cuts, cuts[1:])
    ]

    def parts_first(side):
        starts = [k * channels + j * width for j in range(chunks) for k in range(2)]
        return jnp.concatenate([side[:, at : at + width] for at in starts], axis=1)

    give = jnp.where(y == 0, parts_first(sides[1]), parts_first(sides[0]))
    near_z = [flip(w, "ctx", 4) for w in near]
    take = flip(give, "tp", 2)
    near_x = [flip(w, "ctx", 1) for w in near]
    take_z = [flip(take[:, 2 * j * width : 2 * (j + 1) * width], "ctx", 4) for j in range(chunks)]
    take_x = flip(take, "ctx", 1)
    near_zx = [flip(w, "ctx", 1) for w in near_z]
    take_zx = [flip(take_z[j], "ctx", 1) for j in range(chunks)]

    moves = {"gate_q": [], "gate_r": [], "gate_1": [], "gate_2": []}
    for ci in range(ctx):
        for ti in range(tp):
            source, over = ci * tp + ti, (ci ^ 2) * tp
            if (ti & 1) == ((ci >> 1) & 1):
                moves["gate_q"].append((source, ci * tp + (ti ^ 1)))
                moves["gate_1"].append((source, ci * tp + (ti ^ 3)))
                moves["gate_2"].append((source, ci * tp + (ti ^ 2)))
            else:
                moves["gate_q"].append((source, over + ti))
                moves["gate_r"].append((source, over + (ti ^ 1)))
                moves["gate_1"].append((source, over + (ti ^ 2)))
                moves["gate_2"].append((source, over + (ti ^ 3)))

    def move(value, name):
        return lax.ppermute(value, ("ctx", "tp"), moves[name])

    gated = (
        turns,
        move(leaves, "gate_q"),
        move(turns, "gate_r"),
        move(leaves, "gate_1"),
        move(turns, "gate_2"),
    )

    rows = residual.shape[0]
    outs = []
    for j in range(chunks):
        weights = [(w, CORE_FIRST) for w in near] + [(take, PART_FIRST)]
        weights += [(w, CORE_FIRST) for w in near_x] + [(take_x, PART_FIRST)]
        weights += [(w, CORE_FIRST) for w in near_z] + [(take_z[j], ONE_PART)]
        weights += [(w, CORE_FIRST) for w in near_zx] + [(take_zx[j], ONE_PART)]
        theirs, ours = cube_product(flags, gated, weights, piece, width, j)
        total = ours + flip(theirs, "tp", 1).astype(jnp.float32)
        pair = flip(total[rows:].astype(jnp.bfloat16), "ctx", 2)
        base = residual[:, j * width : (j + 1) * width].astype(jnp.float32)
        outs.append((base + (total[:rows] + pair.astype(jnp.float32))).astype(jnp.bfloat16))
    return jnp.concatenate(outs, axis=1)


def on_device(features, short_filter, log_decay, residue, residual, out_weight):
    ctx, tp = lax.axis_size("ctx"), lax.axis_size("tp")
    piece = out_weight.shape[0]
    if cube_shaped(ctx, tp) and piece == LANES:
        core, y, x, zp, zh = cube_place()
        stays = (core == zp).astype(jnp.int32)
        same = (y == zh).astype(jnp.int32)
        flags = jnp.stack([core, x, y, same, core ^ stays, stays]).astype(jnp.int32)
        leaves, turns = gated_blocks(features, short_filter, log_decay, residue, flags, 2)
        return project_cube(leaves, turns, flags, residual, out_weight, CHUNKS)
    flags = jnp.zeros((1,), jnp.int32)
    (gated,) = gated_blocks(features, short_filter, log_decay, residue, flags, 1)
    return project_gathered(gated, residual, out_weight)


def cube_shaped(ctx, tp):
    return tp == 4 and ctx == 2 * tp


def solution(mesh):
    return jax.shard_map(
        on_device,
        mesh=mesh,
        in_specs=(
            P("ctx", None, "tp"),
            P(None, None, "tp"),
            P(None, "tp"),
            P(None, "tp"),
            P("ctx", "tp"),
            P(("ctx", "tp"), None),
        ),
        out_specs=P("ctx", "tp"),
        check_vma=False,
    )
```

```python
import functools

import jax
import jax.numpy as jnp
from jax import lax
from jax.experimental import pallas as pl
from jax.experimental.pallas import tpu as pltpu
from jax.sharding import PartitionSpec as P


LANES = 128
CHUNKS = 2
UNROLL = 32
CUTS = (3,)
CORE_FIRST, PART_FIRST, ONE_PART = range(3)
SEGS = 8


def row(ref_value, n):
    return jnp.broadcast_to(ref_value[n : n + 1, :], (SEGS, ref_value.shape[1]))


def shifted(value, halo_row):
    lane_row = lax.broadcasted_iota(jnp.int32, value.shape, 0)
    return jnp.where(lane_row == 0, halo_row, pltpu.roll(value, 1, 0))


def history(tokens, halo, stream, lanes, seg_len, filter_len):
    rim = halo[stream, :, lanes].astype(jnp.float32)
    past = []
    for back in range(1, filter_len):
        last = tokens[pl.ds(seg_len - back, SEGS, stride=seg_len), :]
        past.append(shifted(last, rim[filter_len - 1 - back : filter_len - back, :]))
    return past


def taps_of(taps, stream, lanes, filter_len):
    values = taps[stream, :, lanes]
    return [row(values, j) for j in range(filter_len)]


def filter_step(now, past, taps):
    total = taps[0] * now
    for tap, old in zip(taps[1:], past):
        total = total + tap * old
    return total, [now] + past[:-1]


def scan_kernel(
    seg_len, feats, halo, taps, decay, end, before, k_rows, v_rows
):
    modes, channels = decay.shape
    filter_len = taps.shape[1]
    seg = lax.broadcasted_iota(jnp.int32, (SEGS, LANES), 0)

    def one_group(group, _):
        lanes = pl.ds(pl.multiple_of(group * LANES, LANES), LANES)
        rate = decay[:, lanes]
        per_token = jnp.exp(-rate)
        step = [row(per_token, n) for n in range(modes)]
        k_rows[...] = feats[1, :, lanes].astype(jnp.float32)
        v_rows[...] = feats[2, :, lanes].astype(jnp.float32)
        k_taps = taps_of(taps, 1, lanes, filter_len)
        v_taps = taps_of(taps, 2, lanes, filter_len)

        def one_token(i, carry):
            states, k_past, v_past = carry
            at = pl.ds(i, SEGS, stride=seg_len)
            k, k_past = filter_step(k_rows[at, :], k_past, k_taps)
            v, v_past = filter_step(v_rows[at, :], v_past, v_taps)
            drive = k * v
            states = [a * s + drive for a, s in zip(step, states)]
            return states, k_past, v_past

        zero = jnp.zeros((SEGS, LANES), jnp.float32)
        states, _, _ = lax.fori_loop(
            0,
            seg_len,
            one_token,
            (
                [zero] * modes,
                history(k_rows, halo, 1, lanes, seg_len, filter_len),
                history(v_rows, halo, 2, lanes, seg_len, filter_len),
            ),
            unroll=UNROLL,
        )
        hop = 1
        while hop < SEGS:
            weight = jnp.exp(-rate * float(seg_len * hop))
            states = [
                s + row(weight, n) * jnp.where(seg >= hop, pltpu.roll(s, hop, 0), 0.0)
                for n, s in enumerate(states)
            ]
            hop *= 2
        for n, s in enumerate(states):
            end[n : n + 1, lanes] = s[SEGS - 1 :, :]
            before[n, :, lanes] = jnp.where(seg >= 1, pltpu.roll(s, 1, 0), 0.0)
        return 0

    lax.fori_loop(0, channels // LANES, one_group, 0)


def local_kernel(
    seg_len, feats, halo, taps, decay, residue, before, gate, local, q_rows, k_rows, v_rows
):
    modes, channels = decay.shape
    filter_len = taps.shape[1]

    def one_group(group, _):
        lanes = pl.ds(pl.multiple_of(group * LANES, LANES), LANES)
        per_token = jnp.exp(-decay[:, lanes])
        weights = residue[:, lanes]
        q_rows[...] = feats[0, :, lanes].astype(jnp.float32)
        step = [row(per_token, n) for n in range(modes)]
        gain = [row(weights, n) for n in range(modes)]
        k_rows[...] = feats[1, :, lanes].astype(jnp.float32)
        v_rows[...] = feats[2, :, lanes].astype(jnp.float32)
        q_taps = taps_of(taps, 0, lanes, filter_len)
        k_taps = taps_of(taps, 1, lanes, filter_len)
        v_taps = taps_of(taps, 2, lanes, filter_len)

        def one_token(i, carry):
            states, q_past, k_past, v_past = carry
            at = pl.ds(i, SEGS, stride=seg_len)
            now, q_past = filter_step(q_rows[at, :], q_past, q_taps)
            k, k_past = filter_step(k_rows[at, :], k_past, k_taps)
            v, v_past = filter_step(v_rows[at, :], v_past, v_taps)
            gate[i, :, lanes] = now
            drive = k * v
            states = [a * s + drive for a, s in zip(step, states)]
            local[i, :, lanes] = tree_sum([r * s for r, s in zip(gain, states)])
            return states, q_past, k_past, v_past

        lax.fori_loop(
            0,
            seg_len,
            one_token,
            (
                [before[n, :, lanes] for n in range(modes)],
                history(q_rows, halo, 0, lanes, seg_len, filter_len),
                history(k_rows, halo, 1, lanes, seg_len, filter_len),
                history(v_rows, halo, 2, lanes, seg_len, filter_len),
            ),
            unroll=UNROLL,
        )
        return 0

    lax.fori_loop(0, channels // LANES, one_group, 0)


def tree_sum(terms):
    while len(terms) > 1:
        terms = [a + b for a, b in zip(terms[::2], terms[1::2])] + terms[len(terms) & ~1 :]
    return terms[0]


def output_kernel(seg_len, parts, flags, decay, residue, gate, local, incoming, *refs):
    outs, rows = refs[:parts], refs[parts]
    modes, channels = decay.shape
    seg = lax.broadcasted_iota(jnp.int32, (SEGS, LANES), 0).astype(jnp.float32)

    def one_group(group, _):
        lanes = pl.ds(pl.multiple_of(group * LANES, LANES), LANES)
        rate = decay[:, lanes]
        per_token = jnp.exp(-rate)
        entering = residue[:, lanes] * incoming[:, lanes]
        step = [row(per_token, n) for n in range(modes)]
        since = seg * float(seg_len) + 1.0
        terms = [jnp.exp(-row(rate, n) * since) * row(entering, n) for n in range(modes)]

        def one_token(i, terms):
            total = local[i, :, lanes] + tree_sum(terms)
            rows[pl.ds(i, SEGS, stride=seg_len), :] = gate[i, :, lanes] * total
            return [a * term for a, term in zip(step, terms)]

        lax.fori_loop(0, seg_len, one_token, terms, unroll=UNROLL)
        place = pl.ds(pl.multiple_of((group // parts) * LANES, LANES), LANES)
        value = rows[...].astype(jnp.bfloat16)
        turned = jnp.bitwise_xor(lax.rem(group, parts), flags[4] if parts > 1 else 0)
        for k in range(parts):

            @pl.when(turned == k)
            def _(k=k):
                outs[k][:, place] = value

        return 0

    lax.fori_loop(0, channels // LANES, one_group, 0)


def flip(value, axis, bit):
    count = lax.axis_size(axis)
    return lax.ppermute(value, axis, [(i, i ^ bit) for i in range(count)])


def entering_state(end, log_decay, tok_rows):
    place = lax.axis_index("ctx")
    count = lax.axis_size("ctx")
    decay_over = lambda tokens: jnp.exp(-log_decay * tokens)
    prefix = jnp.zeros_like(end)
    total = end
    bit = 2
    while bit < count:
        other = flip(total, "ctx", bit)
        upper = (place & bit) != 0
        covered = (place & (bit - 2)).astype(jnp.float32) * float(tok_rows)
        prefix = prefix + jnp.where(upper, decay_over(covered) * other, 0.0)
        first = jnp.where(upper, other, total)
        second = jnp.where(upper, total, other)
        total = decay_over(float(tok_rows * bit)) * first + second
        bit *= 2
    even = (place & 1) == 0
    message = jnp.where(even, decay_over(float(2 * tok_rows)) * prefix + end, prefix)
    other = flip(message, "ctx", 1)
    return decay_over(float(tok_rows)) * prefix + other


def in_vmem(kernel, out_shape, inputs, scratch, flops, flags=None):
    arrays = [pltpu.with_memory_space_constraint(a, pltpu.VMEM) for a in inputs]
    specs = [pl.BlockSpec(memory_space=pltpu.VMEM)] * len(arrays)
    if flags is not None:
        arrays, specs = [flags] + arrays, [pl.BlockSpec(memory_space=pltpu.SMEM)] + specs
    single = not isinstance(out_shape, tuple)
    return pl.pallas_call(
        kernel,
        out_shape=out_shape,
        in_specs=specs,
        out_specs=pl.BlockSpec(memory_space=pltpu.VMEM)
        if single
        else (pl.BlockSpec(memory_space=pltpu.VMEM),) * len(out_shape),
        scratch_shapes=scratch,
        compiler_params=pltpu.CompilerParams(vmem_limit_bytes=8 << 20),
        cost_estimate=pl.CostEstimate(flops=flops, bytes_accessed=flops // 200, transcendentals=0),
    )(*arrays)


def gated_blocks(features, short_filter, log_decay, residue, flags, parts):
    tok_rows, _, channels = features.shape
    filter_len = short_filter.shape[1]
    modes = log_decay.shape[0]
    seg_len = tok_rows // SEGS
    count = lax.axis_size("ctx")
    rim = lax.ppermute(
        features[tok_rows - (filter_len - 1) :],
        "ctx",
        [(i, i + 1) for i in range(count - 1)],
    )
    feats = jnp.transpose(features, (1, 0, 2))
    halo = jnp.transpose(rim, (1, 0, 2))
    tokens = pltpu.VMEM((seg_len, SEGS, channels), jnp.float32)
    states = pltpu.VMEM((modes, channels), jnp.float32)
    starts = pltpu.VMEM((modes, SEGS, channels), jnp.float32)
    lane_rows = pltpu.VMEM((tok_rows, LANES), jnp.float32)
    flops = 400 * tok_rows * channels * modes
    inputs = (feats, halo, short_filter, log_decay)
    end, before = in_vmem(
        functools.partial(scan_kernel, seg_len), (states, starts), inputs, [lane_rows] * 2, flops
    )
    incoming = entering_state(end, log_decay, tok_rows)
    gate, local = in_vmem(
        functools.partial(local_kernel, seg_len),
        (tokens, tokens),
        (*inputs, residue, before),
        [lane_rows] * 3,
        flops,
    )
    out = pltpu.VMEM((tok_rows, channels // parts), jnp.bfloat16)
    return in_vmem(
        functools.partial(output_kernel, seg_len, parts),
        (out,) * parts,
        (log_decay, residue, gate, local, incoming),
        [lane_rows],
        flops,
        flags,
    )


def project_gathered(gated, residual, out_weight):
    columns = lax.all_to_all(out_weight, "tp", split_axis=1, concat_axis=0, tiled=True)
    weight = lax.all_gather(columns, "ctx", axis=0, tiled=True)
    rows = lax.all_gather(gated, "tp", axis=1, tiled=True)
    projected = jnp.dot(rows, weight, preferred_element_type=jnp.float32)
    return (residual.astype(jnp.float32) + projected).astype(jnp.bfloat16)


def fill_left(left, flags, piece, near_plane, far_plane):
    x, y = flags[1], flags[2]
    rows = near_plane[0].shape[0]
    for plane, sources in enumerate((near_plane, far_plane)):
        for token, source in enumerate(sources):
            for xr in range(2):
                for yr in range(2):
                    at = jnp.bitwise_xor(x, xr) * 2 + jnp.bitwise_xor(y, yr)
                    place = ((plane * 2 + xr) * 2 + yr) * piece
                    left[pl.ds(token * rows, rows), pl.ds(place, piece)] = source[
                        :, pl.ds(pl.multiple_of(at * piece, piece), piece)
                    ]


def cube_kernel(piece, orders, part, flags, kept, from_q, from_r, from_1, from_2, across, *refs):
    weights, (theirs, mine, left) = refs[:-3], refs[-3:]
    width = mine.shape[1]
    full = weights[0].shape[1] // 2
    tile = min(width, 512)

    for stays, own, other in (
        (1, (kept, from_q), (from_2, across)),
        (0, (from_q, from_r), (from_1, across)),
    ):
        for same, near_plane, far_plane in ((1, own, other), (0, other, own)):

            @pl.when(jnp.logical_and(flags[3] == same, flags[5] == stays))
            def _(near_plane=near_plane, far_plane=far_plane):
                fill_left(left, flags, piece, near_plane, far_plane)

    for side, out in ((1 - flags[0], theirs), (flags[0], mine)):

        def one_tile(i, _, side=side, out=out):
            def columns(k):
                first = {
                    CORE_FIRST: side * full + part * width,
                    PART_FIRST: (2 * part + side) * width,
                    ONE_PART: side * width,
                }[orders[k]]
                return pl.ds(pl.multiple_of(first + i * tile, tile), tile)

            right = jnp.concatenate([w[:, columns(k)] for k, w in enumerate(weights)], axis=0)
            total = jnp.dot(left[...], right, preferred_element_type=jnp.float32)
            out[:, pl.ds(pl.multiple_of(i * tile, tile), tile)] = total.astype(out.dtype)
            return 0

        lax.fori_loop(0, width // tile, one_tile, 0, unroll=True)


def cube_product(flags, gated, weights, piece, width, part):
    rows = 2 * gated[0].shape[0]
    depth = sum(w.shape[0] for w, _ in weights)
    return in_vmem(
        functools.partial(cube_kernel, piece, [order for _, order in weights], part),
        (pltpu.VMEM((rows, width), jnp.bfloat16), pltpu.VMEM((rows, width), jnp.float32)),
        (*gated, *[w for w, _ in weights]),
        [pltpu.VMEM((rows, depth), jnp.bfloat16)],
        4 * rows * width * depth,
        flags,
    )


def cube_place():
    c, t = lax.axis_index("ctx"), lax.axis_index("tp")
    core, y = t & 1, t >> 1
    x, zp, zh = c & 1, (c >> 1) & 1, c >> 2
    return core, y, x, zp, zh


def project_cube(leaves, turns, flags, residual, out_weight, chunks):
    ctx, tp = lax.axis_size("ctx"), lax.axis_size("tp")
    core, y, _, zp, _ = cube_place()
    piece, columns = out_weight.shape
    channels = columns // tp
    width = channels // chunks

    sides = [out_weight[:, : 2 * channels], out_weight[:, 2 * channels :]]
    cuts = [0] + [piece * k // 8 for k in CUTS] + [piece]
    near = [
        jnp.where(y == 0, sides[0][lo:hi], sides[1][lo:hi]) for lo, hi in zip(cuts, cuts[1:])
    ]

    def parts_first(side):
        starts = [k * channels + j * width for j in range(chunks) for k in range(2)]
        return jnp.concatenate([side[:, at : at + width] for at in starts], axis=1)

    give = jnp.where(y == 0, parts_first(sides[1]), parts_first(sides[0]))
    near_z = [flip(w, "ctx", 4) for w in near]
    take = flip(give, "tp", 2)
    near_x = [flip(w, "ctx", 1) for w in near]
    take_z = [flip(take[:, 2 * j * width : 2 * (j + 1) * width], "ctx", 4) for j in range(chunks)]
    take_x = flip(take, "ctx", 1)
    near_zx = [flip(w, "ctx", 1) for w in near_z]
    take_zx = [flip(take_z[j], "ctx", 1) for j in range(chunks)]

    moves = {"gate_q": [], "gate_r": [], "gate_1": [], "gate_2": []}
    for ci in range(ctx):
        for ti in range(tp):
            source, over = ci * tp + ti, (ci ^ 2) * tp
            if (ti & 1) == ((ci >> 1) & 1):
                moves["gate_q"].append((source, ci * tp + (ti ^ 1)))
                moves["gate_1"].append((source, ci * tp + (ti ^ 3)))
                moves["gate_2"].append((source, ci * tp + (ti ^ 2)))
            else:
                moves["gate_q"].append((source, over + ti))
                moves["gate_r"].append((source, over + (ti ^ 1)))

    def move(value, name):
        return lax.ppermute(value, ("ctx", "tp"), moves[name])

    from_q, from_r = move(leaves, "gate_q"), move(turns, "gate_r")
    from_1, from_2 = move(leaves, "gate_1"), move(turns, "gate_2")
    across = flip(jnp.where(core == zp, from_q, from_r), "tp", 2)
    gated = (turns, from_q, from_r, from_1, from_2, across)

    rows = residual.shape[0]
    out = residual
    for j in range(chunks):
        weights = [(w, CORE_FIRST) for w in near] + [(take, PART_FIRST)]
        weights += [(w, CORE_FIRST) for w in near_x] + [(take_x, PART_FIRST)]
        weights += [(w, CORE_FIRST) for w in near_z] + [(take_z[j], ONE_PART)]
        weights += [(w, CORE_FIRST) for w in near_zx] + [(take_zx[j], ONE_PART)]
        theirs, ours = cube_product(flags, gated, weights, piece, width, j)
        total = ours + flip(theirs, "tp", 1).astype(jnp.float32)
        pair = flip(total[rows:].astype(jnp.bfloat16), "ctx", 2)
        base = residual[:, j * width : (j + 1) * width].astype(jnp.float32)
        value = (base + (total[:rows] + pair.astype(jnp.float32))).astype(jnp.bfloat16)
        out = lax.dynamic_update_slice(out, value, (0, j * width))
    return out


def on_device(features, short_filter, log_decay, residue, residual, out_weight):
    ctx, tp = lax.axis_size("ctx"), lax.axis_size("tp")
    piece = out_weight.shape[0]
    if cube_shaped(ctx, tp) and piece == LANES:
        core, y, x, zp, zh = cube_place()
        stays = (core == zp).astype(jnp.int32)
        same = (y == zh).astype(jnp.int32)
        flags = jnp.stack([core, x, y, same, core ^ stays, stays]).astype(jnp.int32)
        leaves, turns = gated_blocks(features, short_filter, log_decay, residue, flags, 2)
        return project_cube(leaves, turns, flags, residual, out_weight, CHUNKS)
    flags = jnp.zeros((1,), jnp.int32)
    (gated,) = gated_blocks(features, short_filter, log_decay, residue, flags, 1)
    return project_gathered(gated, residual, out_weight)


def cube_shaped(ctx, tp):
    return tp == 4 and ctx == 2 * tp


def solution(mesh):
    return jax.shard_map(
        on_device,
        mesh=mesh,
        in_specs=(
            P("ctx", None, "tp"),
            P(None, None, "tp"),
            P(None, "tp"),
            P(None, "tp"),
            P("ctx", "tp"),
            P(("ctx", "tp"), None),
        ),
        out_specs=P("ctx", "tp"),
        check_vma=False,
    )
```
